128 devices in a mesh: row: 8 (over z, y_hi), col: 4 (over y_lo, core), feat: 4 (over x).
Axes of the slice: x: 4, y: 4 (y_hi: 2, y_lo: 2; y = y_hi * 2 + y_lo), z: 4, core: 2. Of those that a mesh axis runs over, the one named last changes fastest.
Arguments:
- features: bfloat16 [262144, 128], P(('row', 'col'), 'feat'), may hold values from -6 to 6
- tiles: bfloat16 [8, 4, 1536, 128, 128], P('row', 'col', 'feat'), may hold values from 0 to 0.04321289
- tile_row: int32 [8, 4, 1536], P('row', 'col', 'feat'), may hold values from 0 to 255
- tile_col: int32 [8, 4, 1536], P('row', 'col', 'feat'), may hold values from 0 to 511
- tile_count: int32 [8, 4, 4], P('row', 'col', 'feat'), may hold values from 1 to 384, as said below
- weight: bfloat16 [128, 256], replicated, may hold values from -0.5 to 0.5
- bias: float32 [256], replicated, may hold values from -3 to 3
Outputs:
- output: bfloat16 [262144, 256], P(('row', 'col', 'feat'))
The draws below stay inside these ranges and needn't reach their ends.
Inputs may be any that keep to these rules, and one draw needn't show every extreme that they name: `tile_count`: some device has all 384 slots live.
All inputs are finite; a program needn't handle non-finite values.
Results may differ from the reference program's by a relative error of at most 0.02.
Values may be sent and summed in bfloat16 or wider, within the bound.
No kernel may reach another device: no remote copies, remote signals or barrier semaphores. Data moves between devices by JAX's collectives and lax.ppermute only.
A program may use at most 128 MiB of HBM per device.

```python
import math
import jax
import jax.numpy as jnp
import numpy as np
from jax import lax

F = 128
H = 256
TB = 128
NODE_DEV = 2048
TILES_DEV = 384
NODES = 262144
BROWS = 256
BCOLS = 512
SLOTS = 1536
N_ROW = 8
N_COL = 4
N_FEAT = 4


def draw_tile_count(key, part):
    levels = jax.random.randint(key, (N_ROW * N_COL * N_FEAT,), 1, 5)
    counts = jnp.maximum(1, TILES_DEV * levels * levels // 16)
    chosen = jax.random.randint(jax.random.fold_in(key, 7), (), 0, N_ROW * N_COL * N_FEAT)
    counts = counts.at[chosen].set(TILES_DEV)
    return counts.reshape(N_ROW, N_COL, N_FEAT).astype(jnp.int32)


def with_ends(result, stream_key, low, high):
    spot = [jax.random.randint(jax.random.fold_in(stream_key, axis), (), 0, length) for axis, length in enumerate(result.shape)]
    main_axis = result.shape.index(max(result.shape))
    neighbour = spot[:main_axis] + [(spot[main_axis] + 1) % result.shape[main_axis]] + spot[main_axis + 1:]
    return result.at[tuple(spot)].set(low).at[tuple(neighbour)].set(high)


def level_of(stream_key, extent, pieces, least, top_value):
    gain, own = 1.0, jax.random.fold_in(stream_key, 6)
    for axis_at, blocks in pieces:
        draws = jnp.exp(jax.random.uniform(jax.random.fold_in(own, axis_at), (blocks,), jnp.float32, least / len(pieces), top_value / len(pieces)))
        gain = gain * jnp.repeat(draws, extent[axis_at] // blocks).reshape([-1 if axis == axis_at else 1 for axis in range(len(extent))])
    return gain


def rank_bounds(amount, lean):
    loads = [(1 << 20) // math.isqrt(grade ** lean) + 1 for grade in range(1, amount + 1)]
    width = 1 + sum(loads) // (1 << 30)
    return np.cumsum(np.array([max(1, weight // width) for weight in loads]))


def ranked_ids(own_key, shape, amount, skew):
    listing = rank_bounds(amount, skew)
    pick = jax.random.randint(jax.random.fold_in(own_key, 1), shape, 0, int(listing[amount - 1]))
    grade = jnp.searchsorted(jnp.asarray(listing, jnp.int32), pick, side="right")
    return jax.random.permutation(jax.random.fold_in(own_key, 2), amount)[grade].astype(jnp.int32)


def centred(key, extent, spread, limit, cuts=(), kind=jnp.bfloat16):
    array = spread * jax.random.normal(key, extent, jnp.float32)
    if cuts:
        array = array * level_of(key, extent, cuts, -0.22, 0.18)
    return jnp.clip(array, -limit, limit).astype(kind)


def setup_inputs(seed: int = 0) -> dict:
    key_of = jax.random.split(jax.random.key(seed), 8)
    return {
        "features": centred(key_of[0], (NODES, F), 1.0, 6.0, ((0, 32), (1, 4))),
        "tiles": jnp.clip(0.04321289 * jax.random.uniform(key_of[1], (N_ROW, N_COL, SLOTS, TB, TB), jnp.float32) ** level_of(key_of[1], (N_ROW, N_COL, SLOTS, TB, TB), ((0, 8), (1, 4), (2, 4)), -0.2, 0.2), 0.0, 0.04321289).astype(jnp.bfloat16),
        "tile_row": with_ends(ranked_ids(key_of[2], (N_ROW, N_COL, SLOTS), BROWS, 2), jax.random.fold_in(key_of[2], 3), 0, BROWS - 1).astype(jnp.int32),
        "tile_col": with_ends(jax.random.randint(key_of[3], (N_ROW, N_COL, SLOTS), 0, BCOLS), jax.random.fold_in(key_of[3], 1), 0, BCOLS - 1).astype(jnp.int32),
        "tile_count": draw_tile_count(jax.random.fold_in(key_of[7], 71), 0),
        "weight": centred(key_of[5], (F, H), F ** -0.5, 0.5),
        "bias": centred(key_of[6], (H,), 0.5, 3.0, (), jnp.float32),
    }


def device_partial(tile_set, rows, cols, count, src_blocks):
    picked = src_blocks[cols]
    prods = jnp.einsum("tij,tjf->tif", tile_set.astype(jnp.float32), picked.astype(jnp.float32))
    live = jnp.arange(tile_set.shape[0], dtype=jnp.int32) < count
    prods = jnp.where(live[:, None, None], prods, jnp.zeros_like(prods))
    partial_value = jnp.zeros((BROWS, TB, F), jnp.float32).at[rows].add(prods)
    return partial_value.reshape(BROWS * TB, F).astype(jnp.bfloat16)


def reference(features, tiles, tile_row, tile_col, tile_count, weight, bias):
    group = N_FEAT * NODE_DEV
    col_sources = features.reshape(N_ROW, N_COL, group, F).transpose(1, 0, 2, 3).reshape(N_COL, BCOLS, TB, F)
    devs = N_ROW * N_COL * N_FEAT
    tile_all = tiles.reshape(devs, TILES_DEV, TB, TB)
    rows_all = tile_row.reshape(devs, TILES_DEV)
    cols_all = tile_col.reshape(devs, TILES_DEV)
    counts = tile_count.reshape(devs)

    def one_device(index):
        column = (index // N_FEAT) % N_COL
        return device_partial(tile_all[index], rows_all[index], cols_all[index], counts[index], col_sources[column])

    partials = lax.map(one_device, jnp.arange(devs, dtype=jnp.int32))
    agg = partials.astype(jnp.float32).reshape(N_ROW, N_COL * N_FEAT, BROWS * TB, F).sum(axis=1).reshape(NODES, F)
    hidden = jnp.dot(agg.astype(jnp.bfloat16), weight, preferred_element_type=jnp.float32) + bias
    return jax.nn.relu(hidden).astype(jnp.bfloat16)
```

```python
import jax
import jax.numpy as jnp
from jax import lax
from jax.experimental import pallas as pl
from jax.experimental.pallas import tpu as pltpu
from jax.sharding import PartitionSpec as P

LOAD = 32
STEP = 4
NT = (((1,), (1,)), ((), ()))


def aggregate_kernel(
    rows_ref, cols_ref, count_ref, tiles_hbm, src_hbm, out_hbm,
    tiles, src, acc, stage, tile_sem, src_sem, out_sem,
):
    side = tiles.shape[-1]
    per_row = src.shape[-1] // side
    count = count_ref[0]
    loads = (count + LOAD - 1) // LOAD

    def tile_copy(i):
        part = pl.ds(pl.multiple_of(i * LOAD, LOAD), LOAD)
        return pltpu.make_async_copy(tiles_hbm.at[part], tiles.at[part], tile_sem.at[i])

    def src_copy(r):
        return pltpu.make_async_copy(src_hbm.at[r], src.at[r], src_sem.at[r])

    groups = src.shape[0]
    for r in range(groups):
        src_copy(r).start()

    @pl.loop(0, loads)
    def _(i):
        tile_copy(i).start()

    zero_rows = 1024
    zeros = jnp.zeros((zero_rows, side), jnp.float32)

    @pl.loop(0, acc.shape[0] // zero_rows)
    def _(i):
        acc[pl.ds(pl.multiple_of(i * zero_rows, zero_rows), zero_rows), :] = zeros

    for r in range(groups):
        src_copy(r).wait()

    def product(k):
        col = cols_ref[k]
        group = col // per_row
        lane = pl.multiple_of((col % per_row) * side, side)
        block = src[group, :, pl.ds(lane, side)]
        return lax.dot_general(tiles[k], block, NT, preferred_element_type=jnp.float32)

    def add(k, value):
        at = pl.ds(pl.multiple_of(rows_ref[k] * side, side), side)
        acc[at, :] += value

    @pl.loop(0, loads)
    def _(i):
        tile_copy(i).wait()
        first = i * LOAD
        here = jnp.minimum(count - first, LOAD)
        whole = here // STEP

        @pl.loop(0, whole)
        def _(s):
            k = first + s * STEP
            values = [product(k + t) for t in range(STEP)]
            for t in range(STEP):
                add(k + t, values[t])

        @pl.loop(whole * STEP, here)
        def _(s):
            add(first + s, product(first + s))

    chunk = stage.shape[1]
    chunks = acc.shape[0] // chunk

    def out_copy(i):
        slot = i % 2
        part = pl.ds(pl.multiple_of(i * chunk, chunk), chunk)
        return pltpu.make_async_copy(stage.at[slot], out_hbm.at[part], out_sem.at[slot])

    for i in range(chunks):
        if i >= 2:
            out_copy(i - 2).wait()
        stage[i % 2] = acc[i * chunk : (i + 1) * chunk, :].astype(jnp.bfloat16)
        out_copy(i).start()
    for i in range(chunks - 2, chunks):
        out_copy(i).wait()


def aggregate(tiles, rows, cols, count, src, out_rows):
    slots, side, _ = tiles.shape
    any_space = pl.BlockSpec(memory_space=pl.ANY)
    return pl.pallas_call(
        aggregate_kernel,
        out_shape=jax.ShapeDtypeStruct((out_rows, side), jnp.bfloat16),
        grid_spec=pltpu.PrefetchScalarGridSpec(
            num_scalar_prefetch=3,
            grid=(1,),
            in_specs=[any_space, any_space],
            out_specs=any_space,
            scratch_shapes=[
                pltpu.VMEM(tiles.shape, jnp.bfloat16),
                pltpu.VMEM(src.shape, jnp.bfloat16),
                pltpu.VMEM((out_rows, side), jnp.float32),
                pltpu.VMEM((2, 2048, side), jnp.bfloat16),
                pltpu.SemaphoreType.DMA((slots // LOAD,)),
                pltpu.SemaphoreType.DMA((src.shape[0],)),
                pltpu.SemaphoreType.DMA((2,)),
            ],
        ),
        compiler_params=pltpu.CompilerParams(vmem_limit_bytes=56 * 2**20),
        name="aggregate",
    )(rows, cols, count, tiles, src)


def body(features, tiles, tile_row, tile_col, tile_count, weight, bias):
    n_row, n_feat = lax.axis_size("row"), lax.axis_size("feat")
    group = features.shape[0]
    node_dev = group // n_feat
    src = lax.all_gather(features.T, ("row", "feat")).reshape(n_row, -1, group)
    slots, side = tiles.shape[2], tiles.shape[3]
    partial = aggregate(
        tiles.reshape(slots, side, side),
        tile_row.reshape(slots),
        tile_col.reshape(slots),
        tile_count.reshape(1),
        src,
        lax.axis_size("col") * n_feat * node_dev,
    )
    agg = lax.psum_scatter(partial, ("col", "feat"), scatter_dimension=0, tiled=True)
    hidden = jnp.dot(agg, weight, preferred_element_type=jnp.float32) + bias
    return jax.nn.relu(hidden).astype(jnp.bfloat16)


def solution(mesh):
    placed = (
        P(("row", "col"), "feat"),
        P("row", "col", "feat", None, None),
        P("row", "col", "feat"),
        P("row", "col", "feat"),
        P("row", "col", "feat"),
        P(),
        P(),
    )
    return jax.shard_map(
        body, mesh=mesh, in_specs=placed, out_specs=P(("row", "col", "feat"), None), check_vma=False
    )
```

```python
import jax
import jax.numpy as jnp
from jax import lax
from jax.experimental import pallas as pl
from jax.experimental.pallas import tpu as pltpu
from jax.sharding import Mesh
from jax.sharding import PartitionSpec as P

LOAD = 32
STEP = 4
EARLY = 20
FIRST_X = 1024
NT = (((1,), (1,)), ((), ()))
NAMES = ("rz", "ry", "cy", "cc", "fx")


def aggregate_kernel(
    rows_ref, cols_ref, info_ref, tiles_hbm, p0, p1, q0, q1, keep_a, keep_b, send_a, send_b,
    tiles, src, acc, stage, tile_sem, src_sem, out_sem,
):
    side = tiles.shape[-1]
    per_row = src.shape[-1] // side
    count, ry, cy, cc, fx = (info_ref[i] for i in range(5))
    loads = (count + LOAD - 1) // LOAD

    def tile_copy(i):
        part = pl.ds(pl.multiple_of(i * LOAD, LOAD), LOAD)
        return pltpu.make_async_copy(tiles_hbm.at[part], tiles.at[part], tile_sem.at[i])

    early = p0.shape[-1]
    src_copies = []
    for n, (ref, plane, lanes) in enumerate(
        (
            (p0, ry, pl.ds(0, early)),
            (p1, 1 - ry, pl.ds(0, early)),
            (q0, ry, pl.ds(early, q0.shape[-1])),
            (q1, 1 - ry, pl.ds(early, q1.shape[-1])),
        )
    ):
        for z in range(ref.shape[0]):
            src_copies.append(
                pltpu.make_async_copy(
                    ref.at[z], src.at[2 * z + plane, :, lanes], src_sem.at[4 * n + z]
                )
            )
    for copy in src_copies:
        copy.start()

    @pl.loop(0, loads)
    def _(i):
        tile_copy(i).start()

    zero_rows = 1024
    zeros = jnp.zeros((zero_rows, side), jnp.float32)

    @pl.loop(0, acc.shape[0] // zero_rows)
    def _(i):
        acc[pl.ds(pl.multiple_of(i * zero_rows, zero_rows), zero_rows), :] = zeros

    for copy in src_copies:
        copy.wait()

    def product(k):
        col = cols_ref[k]
        group = col // per_row
        lane = pl.multiple_of((col % per_row) * side, side)
        block = src[group, :, pl.ds(lane, side)]
        return lax.dot_general(tiles[k], block, NT, preferred_element_type=jnp.float32)

    def add(k, value):
        at = pl.ds(pl.multiple_of(rows_ref[k] * side, side), side)
        acc[at, :] += value

    @pl.loop(0, loads)
    def _(i):
        tile_copy(i).wait()
        first = i * LOAD
        here = jnp.minimum(count - first, LOAD)
        whole = here // STEP

        @pl.loop(0, whole)
        def _(s):
            k = first + s * STEP
            values = [product(k + t) for t in range(STEP)]
            for t in range(STEP):
                add(k + t, values[t])

        @pl.loop(whole * STEP, here)
        def _(s):
            add(first + s, product(first + s))

    chunk = stage.shape[1]
    copies = []
    for n in range(16):
        other, y, d = n < 8, 1 - (n // 4) % 2, n % 4
        slot = n % 2
        if n >= 2:
            for copy in copies[n - 2]:
                copy.wait()
        core = 1 - cc if other else cc
        shard = (jnp.bitwise_xor(cy, y) * 2 + core) * 4 + (fx + d) % 4
        stage[slot] = acc[pl.ds(pl.multiple_of(shard * chunk, chunk), chunk), :].astype(jnp.bfloat16)
        out_a, out_b = (send_a, send_b) if other else (keep_a, keep_b)
        copies.append(
            [
                pltpu.make_async_copy(
                    stage.at[slot, pl.ds(0, FIRST_X)], out_a.at[d, y], out_sem.at[slot, 0]
                ),
                pltpu.make_async_copy(
                    stage.at[slot, pl.ds(FIRST_X, chunk - FIRST_X)], out_b.at[y, d], out_sem.at[slot, 1]
                ),
            ]
        )
        for copy in copies[n]:
            copy.start()
    for n in (14, 15):
        for copy in copies[n]:
            copy.wait()


def aggregate(tiles, rows, cols, info, parts, node_dev):
    slots, side, _ = tiles.shape
    any_space = pl.BlockSpec(memory_space=pl.ANY)
    early, group = parts[0].shape[-1], parts[0].shape[-1] + parts[2].shape[-1]
    part_a = jax.ShapeDtypeStruct((4, 2, FIRST_X, side), jnp.bfloat16)
    part_b = jax.ShapeDtypeStruct((2, 4, node_dev - FIRST_X, side), jnp.bfloat16)
    return pl.pallas_call(
        aggregate_kernel,
        out_shape=(part_a, part_b, part_a, part_b),
        grid_spec=pltpu.PrefetchScalarGridSpec(
            num_scalar_prefetch=3,
            grid=(1,),
            in_specs=[any_space] * 5,
            out_specs=(any_space,) * 4,
            scratch_shapes=[
                pltpu.VMEM(tiles.shape, jnp.bfloat16),
                pltpu.VMEM((8, side, group), jnp.bfloat16),
                pltpu.VMEM((16 * node_dev, side), jnp.float32),
                pltpu.VMEM((2, node_dev, side), jnp.bfloat16),
                pltpu.SemaphoreType.DMA((slots // LOAD,)),
                pltpu.SemaphoreType.DMA((16,)),
                pltpu.SemaphoreType.DMA((2, 2)),
            ],
        ),
        compiler_params=pltpu.CompilerParams(vmem_limit_bytes=56 * 2**20),
        name="aggregate",
    )(rows, cols, info, tiles, *parts)


def swap(value, axis):
    return lax.ppermute(value, axis, [(0, 1), (1, 0)])


def shift(value, axis, by):
    n = lax.axis_size(axis)
    return lax.ppermute(value, axis, [(i, (i + by) % n) for i in range(n)])


def total(*values):
    wide = values[0].astype(jnp.float32)
    for value in values[1:]:
        wide = wide + value.astype(jnp.float32)
    return wide


def low(value):
    return value.astype(jnp.bfloat16)


def gather_sources(x):
    early = EARLY * 128
    p, q = x[:, :early], x[:, early:]
    q_other = swap(q, "ry")

    def plane(value):
        return lax.all_gather(value, ("rz", "fx")).reshape(4, -1, value.shape[-1])

    p0 = plane(p)
    p1 = swap(p0, "ry")
    return p0, p1, plane(q), plane(q_other)


def reduce_rows(keep_a, keep_b, send_a, send_b):
    got_b = swap(send_b, "cc")
    got_a = swap(send_a, "cc")
    b = swap(low(total(keep_b[1], got_b[1])), "cy")
    a = [shift(low(total(keep_a[d], got_a[d])), "fx", d) for d in (1, 2, 3)]
    b_here = [low(total(keep_b[0, d], got_b[0, d], b[d])) for d in (1, 2, 3)]
    b_got = [shift(v, "fx", d) for v, d in zip(b_here, (1, 2, 3))]
    a_here = total(keep_a[0], got_a[0], *a)
    a_got = swap(low(a_here[1]), "cy")
    a_sum = a_here[0] + a_got.astype(jnp.float32)
    b_sum = total(keep_b[0, 0], got_b[0, 0], b[0], *b_got)
    return jnp.concatenate([low(a_sum), low(b_sum)], axis=0)


def body(features, tiles, tile_row, tile_col, tile_count, weight, bias):
    node_dev = features.shape[0] // lax.axis_size("fx")
    slots, side = tiles.shape[2], tiles.shape[3]
    place = [lax.axis_index(n) for n in NAMES[1:]]
    info = jnp.stack([tile_count.reshape(())] + [i.astype(jnp.int32) for i in place])
    parts = aggregate(
        tiles.reshape(slots, side, side),
        tile_row.reshape(slots),
        tile_col.reshape(slots),
        info,
        gather_sources(features.T),
        node_dev,
    )
    agg = reduce_rows(*parts)
    hidden = jnp.dot(agg, weight, preferred_element_type=jnp.float32) + bias
    return jax.nn.relu(hidden).astype(jnp.bfloat16)


def solution(mesh):
    fine = Mesh(mesh.devices.reshape(4, 2, 2, 2, 4), NAMES)
    row, col = ("rz", "ry"), ("cy", "cc")
    placed = (
        P(row + col, "fx"),
        P(row, col, "fx", None, None),
        P(row, col, "fx"),
        P(row, col, "fx"),
        P(row, col, "fx"),
        P(),
        P(),
    )
    return jax.shard_map(
        body, mesh=fine, in_specs=placed, out_specs=P(NAMES, None), check_vma=False
    )
```

```python
import functools

import jax
import jax.numpy as jnp
from jax import lax
from jax.experimental import pallas as pl
from jax.experimental.pallas import tpu as pltpu
from jax.sharding import Mesh
from jax.sharding import PartitionSpec as P

LOAD = 32
STEP = 4
EARLY = 25
LATE_X = 29
FIRST_X = 1024
NT = (((1,), (1,)), ((), ()))
NAMES = ("rz", "ry", "cy", "cc", "fx")


def aggregate_kernel(where, n_parts, rows_ref, cols_ref, info_ref, tiles_hbm, *refs):
    parts, (keep_a, keep_b, send_a, send_b) = refs[:n_parts], refs[n_parts : n_parts + 4]
    tiles, src, acc, stage, tile_sem, src_sem, out_sem = refs[n_parts + 4 :]
    side = tiles.shape[-1]
    per_row = src.shape[-1] // side
    count, rz, ry, cy, cc, fx = (info_ref[i] for i in range(6))
    loads = (count + LOAD - 1) // LOAD

    def tile_copy(i):
        part = pl.ds(pl.multiple_of(i * LOAD, LOAD), LOAD)
        return pltpu.make_async_copy(tiles_hbm.at[part], tiles.at[part], tile_sem.at[i])

    src_copies = []
    for ref, (first, offsets) in zip(parts, where):
        for n, (z, y, x) in enumerate(offsets):
            row = jnp.bitwise_and(rz + z, 3) * 2 + jnp.bitwise_xor(ry, y)
            col = jnp.bitwise_and(fx + x, 3)
            to = src.at[row, col, :, pl.ds(first, ref.shape[-1])]
            src_copies.append(pltpu.make_async_copy(ref.at[n], to, src_sem.at[len(src_copies)]))
    for copy in src_copies:
        copy.start()

    @pl.loop(0, loads)
    def _(i):
        tile_copy(i).start()

    zero_rows = 1024
    zeros = jnp.zeros((zero_rows, side), jnp.float32)

    @pl.loop(0, acc.shape[0] // zero_rows)
    def _(i):
        acc[pl.ds(pl.multiple_of(i * zero_rows, zero_rows), zero_rows), :] = zeros

    for copy in src_copies:
        copy.wait()

    def product(k):
        col = cols_ref[k]
        group = col // per_row
        lane = pl.multiple_of((col % per_row) * side, side)
        block = src[group, :, :, pl.ds(lane, side)].reshape(side, side)
        return lax.dot_general(tiles[k], block, NT, preferred_element_type=jnp.float32)

    def add(k, value):
        at = pl.ds(pl.multiple_of(rows_ref[k] * side, side), side)
        acc[at, :] += value

    @pl.loop(0, loads)
    def _(i):
        tile_copy(i).wait()
        first = i * LOAD
        here = jnp.minimum(count - first, LOAD)
        whole = here // STEP

        @pl.loop(0, whole)
        def _(s):
            k = first + s * STEP
            values = [product(k + t) for t in range(STEP)]
            for t in range(STEP):
                add(k + t, values[t])

        @pl.loop(whole * STEP, here)
        def _(s):
            add(first + s, product(first + s))

    chunk = stage.shape[1]
    copies = []
    for n in range(16):
        other, y, d = n < 8, 1 - (n // 4) % 2, n % 4
        slot = n % 2
        if n >= 2:
            for copy in copies[n - 2]:
                copy.wait()
        core = 1 - cc if other else cc
        shard = (jnp.bitwise_xor(cy, y) * 2 + core) * 4 + jnp.bitwise_and(fx + d, 3)
        stage[slot] = acc[pl.ds(pl.multiple_of(shard * chunk, chunk), chunk), :].astype(jnp.bfloat16)
        out_a, out_b = (send_a, send_b) if other else (keep_a, keep_b)
        copies.append(
            [
                pltpu.make_async_copy(
                    stage.at[slot, pl.ds(0, FIRST_X)], out_a.at[d, y], out_sem.at[slot, 0]
                ),
                pltpu.make_async_copy(
                    stage.at[slot, pl.ds(FIRST_X, chunk - FIRST_X)], out_b.at[y, d], out_sem.at[slot, 1]
                ),
            ]
        )
        for copy in copies[n]:
            copy.start()
    for n in (14, 15):
        for copy in copies[n]:
            copy.wait()


def aggregate(tiles, rows, cols, info, parts, node_dev):
    slots, side, _ = tiles.shape
    any_space = pl.BlockSpec(memory_space=pl.ANY)
    arrays, where = [p[0] for p in parts], [p[1:] for p in parts]
    part_a = jax.ShapeDtypeStruct((4, 2, FIRST_X, side), jnp.bfloat16)
    part_b = jax.ShapeDtypeStruct((2, 4, node_dev - FIRST_X, side), jnp.bfloat16)
    return pl.pallas_call(
        functools.partial(aggregate_kernel, where, len(arrays)),
        out_shape=(part_a, part_b, part_a, part_b),
        grid_spec=pltpu.PrefetchScalarGridSpec(
            num_scalar_prefetch=3,
            grid=(1,),
            in_specs=[any_space] * (1 + len(arrays)),
            out_specs=(any_space,) * 4,
            scratch_shapes=[
                pltpu.VMEM(tiles.shape, jnp.bfloat16),
                pltpu.VMEM((8, 4, side // 4, 4 * node_dev), jnp.bfloat16),
                pltpu.VMEM((16 * node_dev, side), jnp.float32),
                pltpu.VMEM((2, node_dev, side), jnp.bfloat16),
                pltpu.SemaphoreType.DMA((slots // LOAD,)),
                pltpu.SemaphoreType.DMA((sum(len(w[1]) for w in where),)),
                pltpu.SemaphoreType.DMA((2, 2)),
            ],
        ),
        compiler_params=pltpu.CompilerParams(vmem_limit_bytes=56 * 2**20),
        name="aggregate",
    )(rows, cols, info, tiles, *arrays)


def swap(value, axis):
    return lax.ppermute(value, axis, [(0, 1), (1, 0)])


def shift(value, axis, by):
    n = lax.axis_size(axis)
    return lax.ppermute(value, axis, [(i, (i + by) % n) for i in range(n)])


def total(*values):
    wide = values[0].astype(jnp.float32)
    for value in values[1:]:
        wide = wide + value.astype(jnp.float32)
    return wide


def low(value):
    return value.astype(jnp.bfloat16)


STEPS = (0, -1, 1, 2)


def ring(value, axis):
    return [value] + [shift(value, axis, -d) for d in STEPS[1:]]


def ring_forward(value, axis):
    before, after = shift(value, axis, 1), shift(value, axis, -1)
    half = value.shape[0] // 2
    return [value, before, after, shift(before[:half], axis, 1), shift(after[half:], axis, -1)]


def gather_sources(x):
    late, last = EARLY * 128, (EARLY + LATE_X) * 128
    p, q = x[:, :late], x[:, late:]
    q = jnp.stack([q, swap(q, "ry")])
    parts = []
    for z, value in zip(STEPS, ring(jnp.stack(ring(p, "fx")), "rz")):
        for y in (0, 1):
            parts.append((swap(value, "ry") if y else value, 0, [(z, y, d) for d in STEPS]))
    a, b = q[:, :, : last - late], q[:, :, last - late :]
    for value, first, x_last in ((a, late, True), (b, last, False)):
        one, two = ("rz", "fx") if x_last else ("fx", "rz")
        done = ring_forward(jnp.stack(ring(value, one)), two)
        for far, near, part in zip((0, -1, 1, 2, 2), (STEPS, STEPS, STEPS, STEPS[:2], STEPS[2:]), done):
            offsets = [
                (d, y, far) if x_last else (far, y, d) for d in near for y in (0, 1)
            ]
            parts.append((part.reshape(-1, *part.shape[2:]), first, offsets))
    return parts


def reduce_rows(keep_a, keep_b, send_a, send_b):
    got_b = swap(send_b, "cc")
    got_a = swap(send_a, "cc")
    b = swap(low(total(keep_b[1], got_b[1])), "cy")
    a = [shift(low(total(keep_a[d], got_a[d])), "fx", d) for d in (1, 2, 3)]
    b_here = [low(total(keep_b[0, d], got_b[0, d], b[d])) for d in (1, 2, 3)]
    b_got = [shift(v, "fx", d) for v, d in zip(b_here, (1, 2, 3))]
    a_here = total(keep_a[0], got_a[0], *a)
    a_got = swap(low(a_here[1]), "cy")
    a_sum = a_here[0] + a_got.astype(jnp.float32)
    b_sum = total(keep_b[0, 0], got_b[0, 0], b[0], *b_got)
    return jnp.concatenate([low(a_sum), low(b_sum)], axis=0)


def body(features, tiles, tile_row, tile_col, tile_count, weight, bias):
    node_dev = features.shape[0] // lax.axis_size("fx")
    slots, side = tiles.shape[2], tiles.shape[3]
    place = [lax.axis_index(n) for n in NAMES]
    info = jnp.stack([tile_count.reshape(())] + [i.astype(jnp.int32) for i in place])
    parts = aggregate(
        tiles.reshape(slots, side, side),
        tile_row.reshape(slots),
        tile_col.reshape(slots),
        info,
        gather_sources(features.T),
        node_dev,
    )
    agg = reduce_rows(*parts)
    hidden = jnp.dot(agg, weight, preferred_element_type=jnp.float32) + bias
    return jax.nn.relu(hidden).astype(jnp.bfloat16)


def solution(mesh):
    fine = Mesh(mesh.devices.reshape(4, 2, 2, 2, 4), NAMES)
    row, col = ("rz", "ry"), ("cy", "cc")
    placed = (
        P(row + col, "fx"),
        P(row, col, "fx", None, None),
        P(row, col, "fx"),
        P(row, col, "fx"),
        P(row, col, "fx"),
        P(),
        P(),
    )
    return jax.shard_map(
        body, mesh=fine, in_specs=placed, out_specs=P(NAMES, None), check_vma=False
    )
```

```python
import functools

import jax
import jax.numpy as jnp
from jax import lax
from jax.experimental import pallas as pl
from jax.experimental.pallas import tpu as pltpu
from jax.sharding import Mesh
from jax.sharding import PartitionSpec as P

LOAD = 32
STEP = 4
EARLY = 18
LATE_X = 23
FIRST_X = 1024
NT = (((1,), (1,)), ((), ()))
NAMES = ("rz", "ry", "cy", "cc", "fx")


def aggregate_kernel(where, n_parts, rows_ref, cols_ref, info_ref, tiles_hbm, *refs):
    parts, (keep_a, keep_b, send_a, send_b) = refs[:n_parts], refs[n_parts : n_parts + 4]
    tiles, src, acc, stage, tile_sem, src_sem, out_sem = refs[n_parts + 4 :]
    side = tiles.shape[-1]
    per_row = src.shape[-1] // side
    count, rz, ry, cy, cc, fx = (info_ref[i] for i in range(6))
    loads = (count + LOAD - 1) // LOAD

    def tile_copy(i):
        part = pl.ds(pl.multiple_of(i * LOAD, LOAD), LOAD)
        return pltpu.make_async_copy(tiles_hbm.at[part], tiles.at[part], tile_sem.at[i])

    src_copies = []
    for ref, (first, offsets) in zip(parts, where):
        for n, (relative, z, y, x) in enumerate(offsets):
            row = (jnp.bitwise_and(rz + z, 3) if relative else z) * 2 + jnp.bitwise_xor(ry, y)
            col = jnp.bitwise_and(fx + x, 3) if relative else x
            to = src.at[row, col, :, pl.ds(first, ref.shape[-1])]
            src_copies.append(pltpu.make_async_copy(ref.at[n], to, src_sem.at[len(src_copies)]))
    for copy in src_copies:
        copy.start()

    @pl.loop(0, loads)
    def _(i):
        tile_copy(i).start()

    zero_rows = 1024
    zeros = jnp.zeros((zero_rows, side), jnp.float32)

    @pl.loop(0, acc.shape[0] // zero_rows)
    def _(i):
        acc[pl.ds(pl.multiple_of(i * zero_rows, zero_rows), zero_rows), :] = zeros

    for copy in src_copies:
        copy.wait()

    def product(k):
        col = cols_ref[k]
        group = col // per_row
        lane = pl.multiple_of((col % per_row) * side, side)
        block = src[group, :, :, pl.ds(lane, side)].reshape(side, side)
        return lax.dot_general(tiles[k], block, NT, preferred_element_type=jnp.float32)

    def add(k, value):
        at = pl.ds(pl.multiple_of(rows_ref[k] * side, side), side)
        acc[at, :] += value

    @pl.loop(0, loads)
    def _(i):
        tile_copy(i).wait()
        first = i * LOAD
        here = jnp.minimum(count - first, LOAD)
        whole = here // STEP

        @pl.loop(0, whole)
        def _(s):
            k = first + s * STEP
            values = [product(k + t) for t in range(STEP)]
            for t in range(STEP):
                add(k + t, values[t])

        @pl.loop(whole * STEP, here)
        def _(s):
            add(first + s, product(first + s))

    chunk = stage.shape[1]
    copies = []
    for n in range(16):
        other, y, d = n < 8, 1 - (n // 4) % 2, n % 4
        slot = n % 2
        if n >= 2:
            for copy in copies[n - 2]:
                copy.wait()
        core = 1 - cc if other else cc
        shard = (jnp.bitwise_xor(cy, y) * 2 + core) * 4 + jnp.bitwise_and(fx + d, 3)
        stage[slot] = acc[pl.ds(pl.multiple_of(shard * chunk, chunk), chunk), :].astype(jnp.bfloat16)
        out_a, out_b = (send_a, send_b) if other else (keep_a, keep_b)
        copies.append(
            [
                pltpu.make_async_copy(
                    stage.at[slot, pl.ds(0, FIRST_X)], out_a.at[d, y], out_sem.at[slot, 0]
                ),
                pltpu.make_async_copy(
                    stage.at[slot, pl.ds(FIRST_X, chunk - FIRST_X)], out_b.at[y, d], out_sem.at[slot, 1]
                ),
            ]
        )
        for copy in copies[n]:
            copy.start()
    for n in (14, 15):
        for copy in copies[n]:
            copy.wait()


def aggregate(tiles, rows, cols, info, parts, node_dev):
    slots, side, _ = tiles.shape
    any_space = pl.BlockSpec(memory_space=pl.ANY)
    arrays, where = [p[0] for p in parts], [p[1:] for p in parts]
    part_a = jax.ShapeDtypeStruct((4, 2, FIRST_X, side), jnp.bfloat16)
    part_b = jax.ShapeDtypeStruct((2, 4, node_dev - FIRST_X, side), jnp.bfloat16)
    return pl.pallas_call(
        functools.partial(aggregate_kernel, where, len(arrays)),
        out_shape=(part_a, part_b, part_a, part_b),
        grid_spec=pltpu.PrefetchScalarGridSpec(
            num_scalar_prefetch=3,
            grid=(1,),
            in_specs=[any_space] * (1 + len(arrays)),
            out_specs=(any_space,) * 4,
            scratch_shapes=[
                pltpu.VMEM(tiles.shape, jnp.bfloat16),
                pltpu.VMEM((8, 4, side // 4, 4 * node_dev), jnp.bfloat16),
                pltpu.VMEM((16 * node_dev, side), jnp.float32),
                pltpu.VMEM((2, node_dev, side), jnp.bfloat16),
                pltpu.SemaphoreType.DMA((slots // LOAD,)),
                pltpu.SemaphoreType.DMA((sum(len(w[1]) for w in where),)),
                pltpu.SemaphoreType.DMA((2, 2)),
            ],
        ),
        compiler_params=pltpu.CompilerParams(vmem_limit_bytes=56 * 2**20),
        name="aggregate",
    )(rows, cols, info, tiles, *arrays)


def swap(value, axis):
    return lax.ppermute(value, axis, [(0, 1), (1, 0)])


def shift(value, axis, by):
    n = lax.axis_size(axis)
    return lax.ppermute(value, axis, [(i, (i + by) % n) for i in range(n)])


def total(*values):
    wide = values[0].astype(jnp.float32)
    for value in values[1:]:
        wide = wide + value.astype(jnp.float32)
    return wide


def low(value):
    return value.astype(jnp.bfloat16)


STEPS = (0, -1, 1, 2)


def ring(value, axis):
    return [value] + [shift(value, axis, -d) for d in STEPS[1:]]


def gather_sources(x):
    late, last = EARLY * 128, (EARLY + LATE_X) * 128
    tie = lax.optimization_barrier
    p = lax.all_gather(x[:, :late], ("rz", "fx")).reshape(4, 4, -1, late)
    q = x[:, late:]
    q = jnp.stack([q, swap(q, "ry")])
    a = jnp.stack(ring(q[:, :, : last - late], "rz"))
    b = jnp.stack(ring(q[:, :, last - late :], "fx"))
    p, a, b = tie((p, a, b))
    p_low = swap(p[:2], "ry")
    sides = [shift(v, axis, by) for v, axis in ((a, "fx"), (b, "rz")) for by in (1, -1)]
    p_low, *sides = tie((p_low, *sides))
    p_high = swap(tie((p[2:], p_low))[0], "ry")
    parts = []
    for value, y, zs in ((p, 0, (0, 1, 2, 3)), (p_low, 1, (0, 1)), (p_high, 1, (2, 3))):
        parts.append((value, 0, [(False, z, y, f) for z in zs for f in range(4)]))
    for value, first, axis, (before, after) in ((a, late, "fx", sides[:2]), (b, last, "rz", sides[2:])):
        done = (value, before, after, shift(before[:2], axis, 1), shift(after[2:], axis, -1))
        for far, near, part in zip((0, -1, 1, 2, 2), (STEPS, STEPS, STEPS, STEPS[:2], STEPS[2:]), done):
            offsets = [
                (True, d, y, far) if axis == "fx" else (True, far, y, d) for d in near for y in (0, 1)
            ]
            parts.append((part, first, offsets))
    return [(v.reshape(-1, *v.shape[2:]), first, offsets) for v, first, offsets in parts]


def reduce_rows(keep_a, keep_b, send_a, send_b):
    got_b = swap(send_b, "cc")
    got_a = swap(send_a, "cc")
    b = swap(low(total(keep_b[1], got_b[1])), "cy")
    a = [shift(low(total(keep_a[d], got_a[d])), "fx", d) for d in (1, 2, 3)]
    b_here = [low(total(keep_b[0, d], got_b[0, d], b[d])) for d in (1, 2, 3)]
    b_got = [shift(v, "fx", d) for v, d in zip(b_here, (1, 2, 3))]
    a_here = total(keep_a[0], got_a[0], *a)
    a_got = swap(low(a_here[1]), "cy")
    a_sum = a_here[0] + a_got.astype(jnp.float32)
    b_sum = total(keep_b[0, 0], got_b[0, 0], b[0], *b_got)
    return jnp.concatenate([low(a_sum), low(b_sum)], axis=0)


def body(features, tiles, tile_row, tile_col, tile_count, weight, bias):
    node_dev = features.shape[0] // lax.axis_size("fx")
    slots, side = tiles.shape[2], tiles.shape[3]
    place = [lax.axis_index(n) for n in NAMES]
    info = jnp.stack([tile_count.reshape(())] + [i.astype(jnp.int32) for i in place])
    parts = aggregate(
        tiles.reshape(slots, side, side),
        tile_row.reshape(slots),
        tile_col.reshape(slots),
        info,
        gather_sources(features.T),
        node_dev,
    )
    agg = reduce_rows(*parts)
    hidden = jnp.dot(agg, weight, preferred_element_type=jnp.float32) + bias
    return jax.nn.relu(hidden).astype(jnp.bfloat16)


def solution(mesh):
    fine = Mesh(mesh.devices.reshape(4, 2, 2, 2, 4), NAMES)
    row, col = ("rz", "ry"), ("cy", "cc")
    placed = (
        P(row + col, "fx"),
        P(row, col, "fx", None, None),
        P(row, col, "fx"),
        P(row, col, "fx"),
        P(row, col, "fx"),
        P(),
        P(),
    )
    return jax.shard_map(
        body, mesh=fine, in_specs=placed, out_specs=P(NAMES, None), check_vma=False
    )
```

```python
import functools

import jax
import jax.numpy as jnp
from jax import lax
from jax.experimental import pallas as pl
from jax.experimental.pallas import tpu as pltpu
from jax.sharding import Mesh
from jax.sharding import PartitionSpec as P

LOAD = 32
STEP = 4
FIRST_X = 1024
NT = (((1,), (1,)), ((), ()))
NAMES = ("rz", "ry", "cy", "cc", "fx")


def aggregate_kernel(where, n_parts, rows_ref, cols_ref, info_ref, tiles_hbm, *refs):
    parts, (keep_a, keep_b, send_a, send_b) = refs[:n_parts], refs[n_parts : n_parts + 4]
    tiles, src, acc, stage, tile_sem, src_sem, out_sem = refs[n_parts + 4 :]
    side = tiles.shape[-1]
    per_row = src.shape[-1] // side
    count, rz, ry, cy, cc, fx = (info_ref[i] for i in range(6))
    loads = (count + LOAD - 1) // LOAD

    def tile_copy(i):
        part = pl.ds(pl.multiple_of(i * LOAD, LOAD), LOAD)
        return pltpu.make_async_copy(tiles_hbm.at[part], tiles.at[part], tile_sem.at[i])

    src_copies = []
    for ref, (first, offsets) in zip(parts, where):
        for n, (z, y, x) in enumerate(offsets):
            row = jnp.bitwise_and(rz + z, 3) * 2 + jnp.bitwise_xor(ry, y)
            col = jnp.bitwise_and(fx + x, 3)
            to = src.at[row, col, :, pl.ds(first, ref.shape[-1])]
            src_copies.append(pltpu.make_async_copy(ref.at[n], to, src_sem.at[len(src_copies)]))
    for copy in src_copies:
        copy.start()

    @pl.loop(0, loads)
    def _(i):
        tile_copy(i).start()

    zero_rows = 1024
    zeros = jnp.zeros((zero_rows, side), jnp.float32)

    @pl.loop(0, acc.shape[0] // zero_rows)
    def _(i):
        acc[pl.ds(pl.multiple_of(i * zero_rows, zero_rows), zero_rows), :] = zeros

    for copy in src_copies:
        copy.wait()

    def product(k):
        col = cols_ref[k]
        group = col // per_row
        lane = pl.multiple_of((col % per_row) * side, side)
        block = src[group, :, :, pl.ds(lane, side)].reshape(side, side)
        return lax.dot_general(tiles[k], block, NT, preferred_element_type=jnp.float32)

    def add(k, value):
        at = pl.ds(pl.multiple_of(rows_ref[k] * side, side), side)
        acc[at, :] += value

    @pl.loop(0, loads)
    def _(i):
        tile_copy(i).wait()
        first = i * LOAD
        here = jnp.minimum(count - first, LOAD)
        whole = here // STEP

        @pl.loop(0, whole)
        def _(s):
            k = first + s * STEP
            values = [product(k + t) for t in range(STEP)]
            for t in range(STEP):
                add(k + t, values[t])

        @pl.loop(whole * STEP, here)
        def _(s):
            add(first + s, product(first + s))

    chunk = stage.shape[1]
    copies = []
    for n in range(16):
        other, y, d = n < 8, 1 - (n // 4) % 2, n % 4
        slot = n % 2
        if n >= 2:
            for copy in copies[n - 2]:
                copy.wait()
        core = 1 - cc if other else cc
        shard = (jnp.bitwise_xor(cy, y) * 2 + core) * 4 + jnp.bitwise_and(fx + d, 3)
        stage[slot] = acc[pl.ds(pl.multiple_of(shard * chunk, chunk), chunk), :].astype(jnp.bfloat16)
        out_a, out_b = (send_a, send_b) if other else (keep_a, keep_b)
        copies.append(
            [
                pltpu.make_async_copy(
                    stage.at[slot, pl.ds(0, FIRST_X)], out_a.at[d, y], out_sem.at[slot, 0]
                ),
                pltpu.make_async_copy(
                    stage.at[slot, pl.ds(FIRST_X, chunk - FIRST_X)], out_b.at[y, d], out_sem.at[slot, 1]
                ),
            ]
        )
        for copy in copies[n]:
            copy.start()
    for n in (14, 15):
        for copy in copies[n]:
            copy.wait()


def aggregate(tiles, rows, cols, info, parts, node_dev):
    slots, side, _ = tiles.shape
    any_space = pl.BlockSpec(memory_space=pl.ANY)
    arrays, where = [p[0] for p in parts], [p[1:] for p in parts]
    part_a = jax.ShapeDtypeStruct((4, 2, FIRST_X, side), jnp.bfloat16)
    part_b = jax.ShapeDtypeStruct((2, 4, node_dev - FIRST_X, side), jnp.bfloat16)
    return pl.pallas_call(
        functools.partial(aggregate_kernel, where, len(arrays)),
        out_shape=(part_a, part_b, part_a, part_b),
        grid_spec=pltpu.PrefetchScalarGridSpec(
            num_scalar_prefetch=3,
            grid=(1,),
            in_specs=[any_space] * (1 + len(arrays)),
            out_specs=(any_space,) * 4,
            scratch_shapes=[
                pltpu.VMEM(tiles.shape, jnp.bfloat16),
                pltpu.VMEM((8, 4, side // 4, 4 * node_dev), jnp.bfloat16),
                pltpu.VMEM((16 * node_dev, side), jnp.float32),
                pltpu.VMEM((2, node_dev, side), jnp.bfloat16),
                pltpu.SemaphoreType.DMA((slots // LOAD,)),
                pltpu.SemaphoreType.DMA((sum(len(w[1]) for w in where),)),
                pltpu.SemaphoreType.DMA((2, 2)),
            ],
        ),
        compiler_params=pltpu.CompilerParams(vmem_limit_bytes=56 * 2**20),
        name="aggregate",
    )(rows, cols, info, tiles, *arrays)


def swap(value, axis):
    return lax.ppermute(value, axis, [(0, 1), (1, 0)])


def shift(value, axis, by):
    n = lax.axis_size(axis)
    return lax.ppermute(value, axis, [(i, (i + by) % n) for i in range(n)])


def total(*values):
    wide = values[0].astype(jnp.float32)
    for value in values[1:]:
        wide = wide + value.astype(jnp.float32)
    return wide


def low(value):
    return value.astype(jnp.bfloat16)


STEPS = (0, -1, 1, 2)


def ring(value, axis):
    return [value] + [shift(value, axis, -d) for d in STEPS[1:]]


def gather_sources(x):
    other = swap(x, "ry")
    half = x.shape[1] // 2
    parts = []
    for first, one, two in ((0, "rz", "fx"), (half, "fx", "rz")):
        lanes = slice(first, first + half)
        value = jnp.stack([jnp.stack(ring(v[:, lanes], one)) for v in (x, other)])
        before, after = shift(value, two, 1), shift(value, two, -1)
        done = (value, before, after, shift(before[:1], two, 1), shift(after[1:], two, -1))
        for far, ys, part in zip((0, -1, 1, 2, 2), ((0, 1), (0, 1), (0, 1), (0,), (1,)), done):
            offsets = [(d, y, far) if two == "fx" else (far, y, d) for y in ys for d in STEPS]
            parts.append((part.reshape(-1, *part.shape[2:]), first, offsets))
    return parts


def reduce_rows(keep_a, keep_b, send_a, send_b):
    got_b = swap(send_b, "cc")
    got_a = swap(send_a, "cc")
    b = swap(low(total(keep_b[1], got_b[1])), "cy")
    a = [shift(low(total(keep_a[d], got_a[d])), "fx", d) for d in (1, 2, 3)]
    b_here = [low(total(keep_b[0, d], got_b[0, d], b[d])) for d in (1, 2, 3)]
    b_got = [shift(v, "fx", d) for v, d in zip(b_here, (1, 2, 3))]
    a_here = total(keep_a[0], got_a[0], *a)
    a_got = swap(low(a_here[1]), "cy")
    a_sum = a_here[0] + a_got.astype(jnp.float32)
    b_sum = total(keep_b[0, 0], got_b[0, 0], b[0], *b_got)
    return jnp.concatenate([low(a_sum), low(b_sum)], axis=0)


def body(features, tiles, tile_row, tile_col, tile_count, weight, bias):
    node_dev = features.shape[0] // lax.axis_size("fx")
    slots, side = tiles.shape[2], tiles.shape[3]
    place = [lax.axis_index(n) for n in NAMES]
    info = jnp.stack([tile_count.reshape(())] + [i.astype(jnp.int32) for i in place])
    parts = aggregate(
        tiles.reshape(slots, side, side),
        tile_row.reshape(slots),
        tile_col.reshape(slots),
        info,
        gather_sources(features.T),
        node_dev,
    )
    agg = reduce_rows(*parts)
    hidden = jnp.dot(agg, weight, preferred_element_type=jnp.float32) + bias
    return jax.nn.relu(hidden).astype(jnp.bfloat16)


def solution(mesh):
    fine = Mesh(mesh.devices.reshape(4, 2, 2, 2, 4), NAMES)
    row, col = ("rz", "ry"), ("cy", "cc")
    placed = (
        P(row + col, "fx"),
        P(row, col, "fx", None, None),
        P(row, col, "fx"),
        P(row, col, "fx"),
        P(row, col, "fx"),
        P(),
        P(),
    )
    return jax.shard_map(
        body, mesh=fine, in_specs=placed, out_specs=P(NAMES, None), check_vma=False
    )
```

```python
import functools

import jax
import jax.numpy as jnp
from jax import lax
from jax.experimental import pallas as pl
from jax.experimental.pallas import tpu as pltpu
from jax.sharding import Mesh
from jax.sharding import PartitionSpec as P

LOAD = 32
STEPS_AT_ONCE = (16, 4, 1)
PACK = 256
FIRST_X = 1024
NT = (((1,), (1,)), ((), ()))
NAMES = ("rz", "ry", "cy", "cc", "fx")


def aggregate_kernel(where, n_parts, rows_ref, cols_ref, info_ref, tiles_hbm, *refs):
    parts, (keep_a, keep_b, send_a, send_b) = refs[:n_parts], refs[n_parts : n_parts + 4]
    tiles, src, acc, stage, tile_sem, src_sem, out_sem = refs[n_parts + 4 :]
    side = tiles.shape[-1]
    per_row = src.shape[-1] // side
    count, rz, ry, cy, cc, fx = (info_ref[i] for i in range(6))
    loads = (count + LOAD - 1) // LOAD

    def tile_copy(i):
        part = pl.ds(pl.multiple_of(i * LOAD, LOAD), LOAD)
        return pltpu.make_async_copy(tiles_hbm.at[part], tiles.at[part], tile_sem.at[i])

    src_copies = []
    for ref, (first, offsets) in zip(parts, where):
        for n, (z, y, x) in enumerate(offsets):
            row = jnp.bitwise_and(rz + z, 3) * 2 + jnp.bitwise_xor(ry, y)
            col = jnp.bitwise_and(fx + x, 3)
            to = src.at[row, col, :, pl.ds(first, ref.shape[-1])]
            src_copies.append(pltpu.make_async_copy(ref.at[n], to, src_sem.at[len(src_copies)]))
    for copy in src_copies:
        copy.start()

    @pl.loop(0, loads)
    def _(i):
        tile_copy(i).start()

    zero_rows = 1024
    zeros = jnp.zeros((zero_rows, side), jnp.float32)

    @pl.loop(0, acc.shape[0] // zero_rows)
    def _(i):
        acc[pl.ds(pl.multiple_of(i * zero_rows, zero_rows), zero_rows), :] = zeros

    for copy in src_copies:
        copy.wait()

    def product(k):
        col = cols_ref[k]
        group = col // per_row
        lane = pl.multiple_of((col % per_row) * side, side)
        block = src[group, :, :, pl.ds(lane, side)].reshape(side, side)
        return lax.dot_general(tiles[k], block, NT, preferred_element_type=jnp.float32)

    def add(k, value):
        at = pl.ds(pl.multiple_of(rows_ref[k] * side, side), side)
        acc[at, :] += value

    @pl.loop(0, loads)
    def _(i):
        tile_copy(i).wait()
        first = i * LOAD
        here = jnp.minimum(count - first, LOAD)
        start = 0
        for width in STEPS_AT_ONCE:
            turns = (here - start) // width

            @pl.loop(0, turns)
            def _(s, start=start, width=width):
                k = first + start + s * width
                values = [product(k + t) for t in range(width)]
                for t in range(width):
                    add(k + t, values[t])

            start = start + turns * width

    slots, chunk = stage.shape[0], stage.shape[1]
    copies = []
    for n in range(16):
        other, y, d = n < 8, 1 - (n // 4) % 2, n % 4
        slot = n % slots
        if n >= slots:
            for copy in copies[n - slots]:
                copy.wait()
        core = 1 - cc if other else cc
        shard = (jnp.bitwise_xor(cy, y) * 2 + core) * 4 + jnp.bitwise_and(fx + d, 3)

        @pl.loop(0, chunk // PACK)
        def _(i, slot=slot, shard=shard):
            at = pl.multiple_of(i * PACK, PACK)
            rows = pl.ds(pl.multiple_of(shard * chunk + at, PACK), PACK)
            stage[slot, pl.ds(at, PACK), :] = acc[rows, :].astype(jnp.bfloat16)

        out_a, out_b = (send_a, send_b) if other else (keep_a, keep_b)
        copies.append(
            [
                pltpu.make_async_copy(
                    stage.at[slot, pl.ds(0, FIRST_X)], out_a.at[d, y], out_sem.at[slot, 0]
                ),
                pltpu.make_async_copy(
                    stage.at[slot, pl.ds(FIRST_X, chunk - FIRST_X)], out_b.at[y, d], out_sem.at[slot, 1]
                ),
            ]
        )
        for copy in copies[n]:
            copy.start()
    for n in range(16 - slots, 16):
        for copy in copies[n]:
            copy.wait()


def aggregate(tiles, rows, cols, info, parts, node_dev):
    slots, side, _ = tiles.shape
    any_space = pl.BlockSpec(memory_space=pl.ANY)
    arrays, where = [p[0] for p in parts], [p[1:] for p in parts]
    part_a = jax.ShapeDtypeStruct((4, 2, FIRST_X, side), jnp.bfloat16)
    part_b = jax.ShapeDtypeStruct((2, 4, node_dev - FIRST_X, side), jnp.bfloat16)
    return pl.pallas_call(
        functools.partial(aggregate_kernel, where, len(arrays)),
        out_shape=(part_a, part_b, part_a, part_b),
        grid_spec=pltpu.PrefetchScalarGridSpec(
            num_scalar_prefetch=3,
            grid=(1,),
            in_specs=[any_space] * (1 + len(arrays)),
            out_specs=(any_space,) * 4,
            scratch_shapes=[
                pltpu.VMEM(tiles.shape, jnp.bfloat16),
                pltpu.VMEM((8, 4, side // 4, 4 * node_dev), jnp.bfloat16),
                pltpu.VMEM((16 * node_dev, side), jnp.float32),
                pltpu.VMEM((4, node_dev, side), jnp.bfloat16),
                pltpu.SemaphoreType.DMA((slots // LOAD,)),
                pltpu.SemaphoreType.DMA((sum(len(w[1]) for w in where),)),
                pltpu.SemaphoreType.DMA((4, 2)),
            ],
        ),
        compiler_params=pltpu.CompilerParams(vmem_limit_bytes=56 * 2**20),
        name="aggregate",
    )(rows, cols, info, tiles, *arrays)


def swap(value, axis):
    return lax.ppermute(value, axis, [(0, 1), (1, 0)])


def shift(value, axis, by):
    n = lax.axis_size(axis)
    return lax.ppermute(value, axis, [(i, (i + by) % n) for i in range(n)])


def total(*values):
    wide = values[0].astype(jnp.float32)
    for value in values[1:]:
        wide = wide + value.astype(jnp.float32)
    return wide


def low(value):
    return value.astype(jnp.bfloat16)


STEPS = (0, -1, 1, 2)


def ring(value, axis):
    return [value] + [shift(value, axis, -d) for d in STEPS[1:]]


def gather_sources(x):
    other = swap(x, "ry")
    half = x.shape[1] // 2
    parts = []
    for first, one, two in ((0, "rz", "fx"), (half, "fx", "rz")):
        lanes = slice(first, first + half)
        value = jnp.stack([jnp.stack(ring(v[:, lanes], one)) for v in (x, other)])
        before, after = shift(value, two, 1), shift(value, two, -1)
        done = (value, before, after, shift(before[:1], two, 1), shift(after[1:], two, -1))
        for far, ys, part in zip((0, -1, 1, 2, 2), ((0, 1), (0, 1), (0, 1), (0,), (1,)), done):
            offsets = [(d, y, far) if two == "fx" else (far, y, d) for y in ys for d in STEPS]
            parts.append((part.reshape(-1, *part.shape[2:]), first, offsets))
    return parts


def reduce_rows(keep_a, keep_b, send_a, send_b):
    got_b = swap(send_b, "cc")
    got_a = swap(send_a, "cc")
    b = swap(low(total(keep_b[1], got_b[1])), "cy")
    a = [shift(low(total(keep_a[d], got_a[d])), "fx", d) for d in (1, 2, 3)]
    b_here = [low(total(keep_b[0, d], got_b[0, d], b[d])) for d in (1, 2, 3)]
    b_got = [shift(v, "fx", d) for v, d in zip(b_here, (1, 2, 3))]
    a_here = total(keep_a[0], got_a[0], *a)
    a_got = swap(low(a_here[1]), "cy")
    a_sum = a_here[0] + a_got.astype(jnp.float32)
    b_sum = total(keep_b[0, 0], got_b[0, 0], b[0], *b_got)
    return jnp.concatenate([low(a_sum), low(b_sum)], axis=0)


def body(features, tiles, tile_row, tile_col, tile_count, weight, bias):
    node_dev = features.shape[0] // lax.axis_size("fx")
    slots, side = tiles.shape[2], tiles.shape[3]
    place = [lax.axis_index(n) for n in NAMES]
    info = jnp.stack([tile_count.reshape(())] + [i.astype(jnp.int32) for i in place])
    parts = aggregate(
        tiles.reshape(slots, side, side),
        tile_row.reshape(slots),
        tile_col.reshape(slots),
        info,
        gather_sources(features.T),
        node_dev,
    )
    agg = reduce_rows(*parts)
    hidden = jnp.dot(agg, weight, preferred_element_type=jnp.float32) + bias
    return jax.nn.relu(hidden).astype(jnp.bfloat16)


def solution(mesh):
    fine = Mesh(mesh.devices.reshape(4, 2, 2, 2, 4), NAMES)
    row, col = ("rz", "ry"), ("cy", "cc")
    placed = (
        P(row + col, "fx"),
        P(row, col, "fx", None, None),
        P(row, col, "fx"),
        P(row, col, "fx"),
        P(row, col, "fx"),
        P(),
        P(),
    )
    return jax.shard_map(
        body, mesh=fine, in_specs=placed, out_specs=P(NAMES, None), check_vma=False
    )
```

```python
import functools

import jax
import jax.numpy as jnp
from jax import lax
from jax.experimental import pallas as pl
from jax.experimental.pallas import tpu as pltpu
from jax.sharding import Mesh
from jax.sharding import PartitionSpec as P

LOAD = 32
STEPS_AT_ONCE = (16, 4, 1)
PACK = 256
FIRST_X = 1024
NT = (((1,), (1,)), ((), ()))
NAMES = ("rz", "ry", "cy", "cc", "fx")


def aggregate_kernel(where, n_parts, rows_ref, cols_ref, info_ref, tiles_hbm, *refs):
    parts, (keep_a, keep_b, send_a, send_b) = refs[:n_parts], refs[n_parts : n_parts + 4]
    tiles, src, acc, stage, tile_sem, src_sem, out_sem = refs[n_parts + 4 :]
    side = tiles.shape[-1]
    per_row = src.shape[-1] // side
    count, rz, ry, cy, cc, fx = (info_ref[i] for i in range(6))
    loads = (count + LOAD - 1) // LOAD

    def tile_copy(i):
        part = pl.ds(pl.multiple_of(i * LOAD, LOAD), LOAD)
        return pltpu.make_async_copy(tiles_hbm.at[part], tiles.at[part], tile_sem.at[i])

    src_copies = []
    for ref, (first, offsets) in zip(parts, where):
        for n, (z, y, x) in enumerate(offsets):
            row = jnp.bitwise_and(rz + z, 3) * 2 + jnp.bitwise_xor(ry, y)
            col = jnp.bitwise_and(fx + x, 3)
            to = src.at[row, col, :, pl.ds(first, ref.shape[-1])]
            src_copies.append(pltpu.make_async_copy(ref.at[n], to, src_sem.at[len(src_copies)]))
    for copy in src_copies:
        copy.start()

    @pl.loop(0, loads)
    def _(i):
        tile_copy(i).start()

    zero_rows = 1024
    zeros = jnp.zeros((zero_rows, side), jnp.float32)

    @pl.loop(0, acc.shape[0] // zero_rows)
    def _(i):
        acc[pl.ds(pl.multiple_of(i * zero_rows, zero_rows), zero_rows), :] = zeros

    for copy in src_copies:
        copy.wait()

    def product(k):
        col = cols_ref[k]
        group = col // per_row
        lane = pl.multiple_of((col % per_row) * side, side)
        block = src[group, :, :, pl.ds(lane, side)].reshape(side, side)
        return lax.dot_general(tiles[k], block, NT, preferred_element_type=jnp.float32)

    def add(k, value):
        at = pl.ds(pl.multiple_of(rows_ref[k] * side, side), side)
        acc[at, :] += value

    @pl.loop(0, loads)
    def _(i):
        tile_copy(i).wait()
        first = i * LOAD
        here = jnp.minimum(count - first, LOAD)
        start = 0
        for width in STEPS_AT_ONCE:
            turns = (here - start) // width

            @pl.loop(0, turns)
            def _(s, start=start, width=width):
                k = first + start + s * width
                values = [product(k + t) for t in range(width)]
                for t in range(width):
                    add(k + t, values[t])

            start = start + turns * width

    slots, chunk = stage.shape[0], stage.shape[1]
    copies = []
    for n in range(16):
        other, y, d = n < 8, 1 - (n // 4) % 2, n % 4
        slot = n % slots
        if n >= slots:
            for copy in copies[n - slots]:
                copy.wait()
        core = 1 - cc if other else cc
        shard = (jnp.bitwise_xor(cy, y) * 2 + core) * 4 + jnp.bitwise_and(fx + d, 3)

        @pl.loop(0, chunk // PACK)
        def _(i, slot=slot, shard=shard):
            at = pl.multiple_of(i * PACK, PACK)
            rows = pl.ds(pl.multiple_of(shard * chunk + at, PACK), PACK)
            stage[slot, pl.ds(at, PACK), :] = acc[rows, :].astype(jnp.bfloat16)

        out_a, out_b = (send_a, send_b) if other else (keep_a, keep_b)
        copies.append(
            [
                pltpu.make_async_copy(
                    stage.at[slot, pl.ds(0, FIRST_X)], out_a.at[d, y], out_sem.at[slot, 0]
                ),
                pltpu.make_async_copy(
                    stage.at[slot, pl.ds(FIRST_X, chunk - FIRST_X)], out_b.at[y, d], out_sem.at[slot, 1]
                ),
            ]
        )
        for copy in copies[n]:
            copy.start()
    for n in range(16 - slots, 16):
        for copy in copies[n]:
            copy.wait()


def aggregate(tiles, rows, cols, info, parts, node_dev):
    slots, side, _ = tiles.shape
    any_space = pl.BlockSpec(memory_space=pl.ANY)
    arrays, where = [p[0] for p in parts], [p[1:] for p in parts]
    part_a = jax.ShapeDtypeStruct((4, 2, FIRST_X, side), jnp.bfloat16)
    part_b = jax.ShapeDtypeStruct((2, 4, node_dev - FIRST_X, side), jnp.bfloat16)
    return pl.pallas_call(
        functools.partial(aggregate_kernel, where, len(arrays)),
        out_shape=(part_a, part_b, part_a, part_b),
        grid_spec=pltpu.PrefetchScalarGridSpec(
            num_scalar_prefetch=3,
            grid=(1,),
            in_specs=[any_space] * (1 + len(arrays)),
            out_specs=(any_space,) * 4,
            scratch_shapes=[
                pltpu.VMEM(tiles.shape, jnp.bfloat16),
                pltpu.VMEM((8, 4, side // 4, 4 * node_dev), jnp.bfloat16),
                pltpu.VMEM((16 * node_dev, side), jnp.float32),
                pltpu.VMEM((4, node_dev, side), jnp.bfloat16),
                pltpu.SemaphoreType.DMA((slots // LOAD,)),
                pltpu.SemaphoreType.DMA((sum(len(w[1]) for w in where),)),
                pltpu.SemaphoreType.DMA((4, 2)),
            ],
        ),
        compiler_params=pltpu.CompilerParams(vmem_limit_bytes=56 * 2**20),
        name="aggregate",
    )(rows, cols, info, tiles, *arrays)


tie = lax.optimization_barrier


def swap(value, axis):
    return lax.ppermute(value, axis, [(0, 1), (1, 0)])


def shift(value, axis, by):
    n = lax.axis_size(axis)
    return lax.ppermute(value, axis, [(i, (i + by) % n) for i in range(n)])


def total(*values):
    wide = values[0].astype(jnp.float32)
    for value in values[1:]:
        wide = wide + value.astype(jnp.float32)
    return wide


def low(value):
    return value.astype(jnp.bfloat16)


STEPS = (0, -1, 1, 2)


def ring(value, axis):
    return [value] + [shift(value, axis, -d) for d in STEPS[1:]]


def gather_sources(x):
    other = swap(x, "ry")
    half = x.shape[1] // 2
    parts = []
    for first, one, two in ((0, "rz", "fx"), (half, "fx", "rz")):
        lanes = slice(first, first + half)
        value = jnp.stack([jnp.stack(ring(v[:, lanes], one)) for v in (x, other)])
        before, after = shift(value, two, 1), shift(value, two, -1)
        done = (value, before, after, shift(before[:1], two, 1), shift(after[1:], two, -1))
        for far, ys, part in zip((0, -1, 1, 2, 2), ((0, 1), (0, 1), (0, 1), (0,), (1,)), done):
            offsets = [(d, y, far) if two == "fx" else (far, y, d) for y in ys for d in STEPS]
            parts.append((part.reshape(-1, *part.shape[2:]), first, offsets))
    return parts


def reduce_rows(keep_a, keep_b, send_a, send_b):
    send_a, got_b = tie((send_a, swap(send_b, "cc")))
    got_a = swap(send_a, "cc")
    b = swap(low(total(keep_b[1], got_b[1])), "cy")
    a = [shift(low(total(keep_a[d], got_a[d])), "fx", d) for d in (1, 2, 3)]
    b_here = [low(total(keep_b[0, d], got_b[0, d], b[d])) for d in (1, 2, 3)]
    b_got = [shift(v, "fx", d) for v, d in zip(b_here, (1, 2, 3))]
    a_here = total(keep_a[0], got_a[0], *a)
    a_got = swap(low(a_here[1]), "cy")
    a_sum = a_here[0] + a_got.astype(jnp.float32)
    b_sum = total(keep_b[0, 0], got_b[0, 0], b[0], *b_got)
    return jnp.concatenate([low(a_sum), low(b_sum)], axis=0)


def body(features, tiles, tile_row, tile_col, tile_count, weight, bias):
    node_dev = features.shape[0] // lax.axis_size("fx")
    slots, side = tiles.shape[2], tiles.shape[3]
    place = [lax.axis_index(n) for n in NAMES]
    info = jnp.stack([tile_count.reshape(())] + [i.astype(jnp.int32) for i in place])
    parts = aggregate(
        tiles.reshape(slots, side, side),
        tile_row.reshape(slots),
        tile_col.reshape(slots),
        info,
        gather_sources(features.T),
        node_dev,
    )
    agg = reduce_rows(*parts)
    hidden = jnp.dot(agg, weight, preferred_element_type=jnp.float32) + bias
    return jax.nn.relu(hidden).astype(jnp.bfloat16)


def solution(mesh):
    fine = Mesh(mesh.devices.reshape(4, 2, 2, 2, 4), NAMES)
    row, col = ("rz", "ry"), ("cy", "cc")
    placed = (
        P(row + col, "fx"),
        P(row, col, "fx", None, None),
        P(row, col, "fx"),
        P(row, col, "fx"),
        P(row, col, "fx"),
        P(),
        P(),
    )
    return jax.shard_map(
        body, mesh=fine, in_specs=placed, out_specs=P(NAMES, None), check_vma=False
    )
```

```python
import functools

import jax
import jax.numpy as jnp
from jax import lax
from jax.experimental import pallas as pl
from jax.experimental.pallas import tpu as pltpu
from jax.sharding import Mesh
from jax.sharding import PartitionSpec as P

LOAD = 32
STEPS_AT_ONCE = (16, 4, 1)
PACK = 256
FIRST_X = 1024
NT = (((1,), (1,)), ((), ()))
NAMES = ("rz", "ry", "cy", "cc", "fx")


def aggregate_kernel(where, n_parts, rows_ref, cols_ref, info_ref, tiles_hbm, *refs):
    parts, (keep_a, keep_b, send_a, send_b) = refs[:n_parts], refs[n_parts : n_parts + 4]
    tiles, src, acc, stage, tile_sem, src_sem, out_sem = refs[n_parts + 4 :]
    side = tiles.shape[-1]
    per_row = src.shape[-1] // side
    count, rz, ry, cy, cc, fx = (info_ref[i] for i in range(6))
    loads = (count + LOAD - 1) // LOAD

    def tile_copy(i):
        part = pl.ds(pl.multiple_of(i * LOAD, LOAD), LOAD)
        return pltpu.make_async_copy(tiles_hbm.at[part], tiles.at[part], tile_sem.at[i])

    src_copies = []
    for ref, (first, offsets) in zip(parts, where):
        for n, (z, y, x) in enumerate(offsets):
            row = jnp.bitwise_and(rz + z, 3) * 2 + jnp.bitwise_xor(ry, y)
            col = jnp.bitwise_and(fx + x, 3)
            to = src.at[row, col, :, pl.ds(first, ref.shape[-1])]
            src_copies.append(pltpu.make_async_copy(ref.at[n], to, src_sem.at[len(src_copies)]))
    for copy in src_copies:
        copy.start()

    @pl.loop(0, loads)
    def _(i):
        tile_copy(i).start()

    zero_rows = 1024
    zeros = jnp.zeros((zero_rows, side), jnp.float32)

    @pl.loop(0, acc.shape[0] // zero_rows)
    def _(i):
        acc[pl.ds(pl.multiple_of(i * zero_rows, zero_rows), zero_rows), :] = zeros

    for copy in src_copies:
        copy.wait()

    def product(k):
        col = cols_ref[k]
        group = col // per_row
        lane = pl.multiple_of((col % per_row) * side, side)
        block = src[group, :, :, pl.ds(lane, side)].reshape(side, side)
        return lax.dot_general(tiles[k], block, NT, preferred_element_type=jnp.float32)

    def add(k, value):
        at = pl.ds(pl.multiple_of(rows_ref[k] * side, side), side)
        acc[at, :] += value

    @pl.loop(0, loads)
    def _(i):
        tile_copy(i).wait()
        first = i * LOAD
        here = jnp.minimum(count - first, LOAD)
        start = 0
        for width in STEPS_AT_ONCE:
            turns = (here - start) // width

            @pl.loop(0, turns)
            def _(s, start=start, width=width):
                k = first + start + s * width
                values = [product(k + t) for t in range(width)]
                for t in range(width):
                    add(k + t, values[t])

            start = start + turns * width

    slots, chunk = stage.shape[0], stage.shape[1]
    copies = []
    for n in range(16):
        other, y, d = n < 8, 1 - (n // 4) % 2, n % 4
        slot = n % slots
        if n >= slots:
            for copy in copies[n - slots]:
                copy.wait()
        core = 1 - cc if other else cc
        shard = (jnp.bitwise_xor(cy, y) * 2 + core) * 4 + jnp.bitwise_and(fx + d, 3)

        @pl.loop(0, chunk // PACK)
        def _(i, slot=slot, shard=shard):
            at = pl.multiple_of(i * PACK, PACK)
            rows = pl.ds(pl.multiple_of(shard * chunk + at, PACK), PACK)
            stage[slot, pl.ds(at, PACK), :] = acc[rows, :].astype(jnp.bfloat16)

        out_a, out_b = (send_a, send_b) if other else (keep_a, keep_b)
        copies.append(
            [
                pltpu.make_async_copy(
                    stage.at[slot, pl.ds(0, FIRST_X)], out_a.at[d, y], out_sem.at[slot, 0]
                ),
                pltpu.make_async_copy(
                    stage.at[slot, pl.ds(FIRST_X, chunk - FIRST_X)], out_b.at[y, d], out_sem.at[slot, 1]
                ),
            ]
        )
        for copy in copies[n]:
            copy.start()
    for n in range(16 - slots, 16):
        for copy in copies[n]:
            copy.wait()


def aggregate(tiles, rows, cols, info, parts, node_dev):
    slots, side, _ = tiles.shape
    any_space = pl.BlockSpec(memory_space=pl.ANY)
    arrays, where = [p[0] for p in parts], [p[1:] for p in parts]
    part_a = jax.ShapeDtypeStruct((4, 2, FIRST_X, side), jnp.bfloat16)
    part_b = jax.ShapeDtypeStruct((2, 4, node_dev - FIRST_X, side), jnp.bfloat16)
    return pl.pallas_call(
        functools.partial(aggregate_kernel, where, len(arrays)),
        out_shape=(part_a, part_b, part_a, part_b),
        grid_spec=pltpu.PrefetchScalarGridSpec(
            num_scalar_prefetch=3,
            grid=(1,),
            in_specs=[any_space] * (1 + len(arrays)),
            out_specs=(any_space,) * 4,
            scratch_shapes=[
                pltpu.VMEM(tiles.shape, jnp.bfloat16),
                pltpu.VMEM((8, 4, side // 4, 4 * node_dev), jnp.bfloat16),
                pltpu.VMEM((16 * node_dev, side), jnp.float32),
                pltpu.VMEM((4, node_dev, side), jnp.bfloat16),
                pltpu.SemaphoreType.DMA((slots // LOAD,)),
                pltpu.SemaphoreType.DMA((sum(len(w[1]) for w in where),)),
                pltpu.SemaphoreType.DMA((4, 2)),
            ],
        ),
        compiler_params=pltpu.CompilerParams(vmem_limit_bytes=56 * 2**20),
        name="aggregate",
    )(rows, cols, info, tiles, *arrays)


tie = lax.optimization_barrier


def swap(value, axis):
    return lax.ppermute(value, axis, [(0, 1), (1, 0)])


def shift(value, axis, by):
    n = lax.axis_size(axis)
    return lax.ppermute(value, axis, [(i, (i + by) % n) for i in range(n)])


def total(*values):
    wide = values[0].astype(jnp.float32)
    for value in values[1:]:
        wide = wide + value.astype(jnp.float32)
    return wide


def low(value):
    return value.astype(jnp.bfloat16)


STEPS = (0, -1, 1, 2)


def ring(value, axis):
    return [value] + [shift(value, axis, -d) for d in STEPS[1:]]


def gather_sources(x):
    half = x.shape[1] // 2
    other = swap(x, "ry")
    a_own, b_own = jnp.stack(ring(x[:, :half], "rz")), jnp.stack(ring(x[:, half:], "fx"))
    a_own, b_own, other = tie((a_own, b_own, other))
    a_near = shift(a_own, "fx", 1), shift(a_own, "fx", -1)
    b_near = shift(b_own, "rz", 1), shift(b_own, "rz", -1)
    a_other, b_other = jnp.stack(ring(other[:, :half], "rz")), jnp.stack(ring(other[:, half:], "fx"))
    a_other, b_other, a_near, b_near = tie((a_other, b_other, a_near, b_near))
    parts = []
    for own, other, near, axis, first in (
        (a_own, a_other, a_near, "fx", 0),
        (b_own, b_other, b_near, "rz", half),
    ):
        before, after = shift(other, axis, 1), shift(other, axis, -1)
        for value, y, far in (
            (own, 0, 0),
            (other, 1, 0),
            (near[0], 0, -1),
            (near[1], 0, 1),
            (before, 1, -1),
            (after, 1, 1),
            (shift(near[0], axis, 1), 0, 2),
            (shift(after, axis, -1), 1, 2),
        ):
            parts.append((value, first, [(d, y, far) if axis == "fx" else (far, y, d) for d in STEPS]))
    return parts


def reduce_rows(keep_a, keep_b, send_a, send_b):
    send_a, got_b = tie((send_a, swap(send_b, "cc")))
    got_a = swap(send_a, "cc")
    b = swap(low(total(keep_b[1], got_b[1])), "cy")
    a = [shift(low(total(keep_a[d], got_a[d])), "fx", d) for d in (1, 2, 3)]
    b_here = [low(total(keep_b[0, d], got_b[0, d], b[d])) for d in (1, 2, 3)]
    b_got = [shift(v, "fx", d) for v, d in zip(b_here, (1, 2, 3))]
    a_here = total(keep_a[0], got_a[0], *a)
    a_got = swap(low(a_here[1]), "cy")
    a_sum = a_here[0] + a_got.astype(jnp.float32)
    b_sum = total(keep_b[0, 0], got_b[0, 0], b[0], *b_got)
    return jnp.concatenate([low(a_sum), low(b_sum)], axis=0)


def body(features, tiles, tile_row, tile_col, tile_count, weight, bias):
    node_dev = features.shape[0] // lax.axis_size("fx")
    slots, side = tiles.shape[2], tiles.shape[3]
    place = [lax.axis_index(n) for n in NAMES]
    info = jnp.stack([tile_count.reshape(())] + [i.astype(jnp.int32) for i in place])
    parts = aggregate(
        tiles.reshape(slots, side, side),
        tile_row.reshape(slots),
        tile_col.reshape(slots),
        info,
        gather_sources(features.T),
        node_dev,
    )
    agg = reduce_rows(*parts)
    hidden = jnp.dot(agg, weight, preferred_element_type=jnp.float32) + bias
    return jax.nn.relu(hidden).astype(jnp.bfloat16)


def solution(mesh):
    fine = Mesh(mesh.devices.reshape(4, 2, 2, 2, 4), NAMES)
    row, col = ("rz", "ry"), ("cy", "cc")
    placed = (
        P(row + col, "fx"),
        P(row, col, "fx", None, None),
        P(row, col, "fx"),
        P(row, col, "fx"),
        P(row, col, "fx"),
        P(),
        P(),
    )
    return jax.shard_map(
        body, mesh=fine, in_specs=placed, out_specs=P(NAMES, None), check_vma=False
    )
```

```python
import functools

import jax
import jax.numpy as jnp
from jax import lax
from jax.experimental import pallas as pl
from jax.experimental.pallas import tpu as pltpu
from jax.sharding import Mesh
from jax.sharding import PartitionSpec as P

LOAD = 32
STEPS_AT_ONCE = (16, 4, 1)
PACK = 256
FIRST_X = 1024
NT = (((1,), (1,)), ((), ()))
NAMES = ("rz", "ry", "cy", "cc", "fx")


def aggregate_kernel(where, n_parts, rows_ref, cols_ref, info_ref, tiles_hbm, *refs):
    parts, (keep_a, keep_b, send_a, send_b) = refs[:n_parts], refs[n_parts : n_parts + 4]
    tiles, src, acc, stage, tile_sem, src_sem, out_sem = refs[n_parts + 4 :]
    side = tiles.shape[-1]
    per_row = src.shape[-1] // side
    count, rz, ry, cy, cc, fx = (info_ref[i] for i in range(6))
    loads = (count + LOAD - 1) // LOAD

    def tile_copy(i):
        part = pl.ds(pl.multiple_of(i * LOAD, LOAD), LOAD)
        return pltpu.make_async_copy(tiles_hbm.at[part], tiles.at[part], tile_sem.at[i])

    src_copies = []
    for ref, (first, offsets) in zip(parts, where):
        for n, (z, y, x) in enumerate(offsets):
            row = jnp.bitwise_and(rz + z, 3) * 2 + jnp.bitwise_xor(ry, y)
            col = jnp.bitwise_and(fx + x, 3)
            to = src.at[row, col, :, pl.ds(first, ref.shape[-1])]
            src_copies.append(pltpu.make_async_copy(ref.at[n], to, src_sem.at[len(src_copies)]))
    for copy in src_copies:
        copy.start()

    @pl.loop(0, loads)
    def _(i):
        tile_copy(i).start()

    zero_rows = 1024
    zeros = jnp.zeros((zero_rows, side), jnp.float32)

    @pl.loop(0, acc.shape[0] // zero_rows)
    def _(i):
        acc[pl.ds(pl.multiple_of(i * zero_rows, zero_rows), zero_rows), :] = zeros

    for copy in src_copies:
        copy.wait()

    def product(k):
        col = cols_ref[k]
        group = col // per_row
        lane = pl.multiple_of((col % per_row) * side, side)
        block = src[group, :, :, pl.ds(lane, side)].reshape(side, side)
        return lax.dot_general(tiles[k], block, NT, preferred_element_type=jnp.float32)

    def add(k, value):
        at = pl.ds(pl.multiple_of(rows_ref[k] * side, side), side)
        acc[at, :] += value

    @pl.loop(0, loads)
    def _(i):
        tile_copy(i).wait()
        first = i * LOAD
        here = jnp.minimum(count - first, LOAD)
        start = 0
        for width in STEPS_AT_ONCE:
            turns = (here - start) // width

            @pl.loop(0, turns)
            def _(s, start=start, width=width):
                k = first + start + s * width
                values = [product(k + t) for t in range(width)]
                for t in range(width):
                    add(k + t, values[t])

            start = start + turns * width

    slots, chunk = stage.shape[0], stage.shape[1]
    copies = []
    for n in range(16):
        other, y, d = n < 8, 1 - (n // 4) % 2, n % 4
        slot = n % slots
        if n >= slots:
            for copy in copies[n - slots]:
                copy.wait()
        core = 1 - cc if other else cc
        shard = (jnp.bitwise_xor(cy, y) * 2 + core) * 4 + jnp.bitwise_and(fx + d, 3)

        @pl.loop(0, chunk // PACK)
        def _(i, slot=slot, shard=shard):
            at = pl.multiple_of(i * PACK, PACK)
            rows = pl.ds(pl.multiple_of(shard * chunk + at, PACK), PACK)
            stage[slot, pl.ds(at, PACK), :] = acc[rows, :].astype(jnp.bfloat16)

        out_a, out_b = (send_a, send_b) if other else (keep_a, keep_b)
        copies.append(
            [
                pltpu.make_async_copy(
                    stage.at[slot, pl.ds(0, FIRST_X)], out_a.at[d, y], out_sem.at[slot, 0]
                ),
                pltpu.make_async_copy(
                    stage.at[slot, pl.ds(FIRST_X, chunk - FIRST_X)], out_b.at[y, d], out_sem.at[slot, 1]
                ),
            ]
        )
        for copy in copies[n]:
            copy.start()
    for n in range(16 - slots, 16):
        for copy in copies[n]:
            copy.wait()


def aggregate(tiles, rows, cols, info, parts, node_dev):
    slots, side, _ = tiles.shape
    any_space = pl.BlockSpec(memory_space=pl.ANY)
    arrays, where = [p[0] for p in parts], [p[1:] for p in parts]
    part_a = jax.ShapeDtypeStruct((4, 2, FIRST_X, side), jnp.bfloat16)
    part_b = jax.ShapeDtypeStruct((2, 4, node_dev - FIRST_X, side), jnp.bfloat16)
    return pl.pallas_call(
        functools.partial(aggregate_kernel, where, len(arrays)),
        out_shape=(part_a, part_b, part_a, part_b),
        grid_spec=pltpu.PrefetchScalarGridSpec(
            num_scalar_prefetch=3,
            grid=(1,),
            in_specs=[any_space] * (1 + len(arrays)),
            out_specs=(any_space,) * 4,
            scratch_shapes=[
                pltpu.VMEM(tiles.shape, jnp.bfloat16),
                pltpu.VMEM((8, 4, side // 4, 4 * node_dev), jnp.bfloat16),
                pltpu.VMEM((16 * node_dev, side), jnp.float32),
                pltpu.VMEM((4, node_dev, side), jnp.bfloat16),
                pltpu.SemaphoreType.DMA((slots // LOAD,)),
                pltpu.SemaphoreType.DMA((sum(len(w[1]) for w in where),)),
                pltpu.SemaphoreType.DMA((4, 2)),
            ],
        ),
        compiler_params=pltpu.CompilerParams(vmem_limit_bytes=56 * 2**20),
        name="aggregate",
    )(rows, cols, info, tiles, *arrays)


tie = lax.optimization_barrier


def swap(value, axis):
    return lax.ppermute(value, axis, [(0, 1), (1, 0)])


def shift(value, axis, by):
    n = lax.axis_size(axis)
    return lax.ppermute(value, axis, [(i, (i + by) % n) for i in range(n)])


def total(*values):
    wide = values[0].astype(jnp.float32)
    for value in values[1:]:
        wide = wide + value.astype(jnp.float32)
    return wide


def low(value):
    return value.astype(jnp.bfloat16)


STEPS = (0, -1, 1, 2)


def ring(value, axis):
    before, after = (shift(value, axis, -d) for d in STEPS[1:3])
    again, before, after = tie((value, before, after))
    return [value, before, after, shift(again, axis, 2)]


def gather_sources(x):
    half = x.shape[1] // 2
    other = swap(x, "ry")
    a_own, b_own = jnp.stack(ring(x[:, :half], "rz")), jnp.stack(ring(x[:, half:], "fx"))
    a_own, b_own = tie((a_own, b_own))
    a_near = shift(a_own, "fx", 1), shift(a_own, "fx", -1)
    b_near = shift(b_own, "rz", 1), shift(b_own, "rz", -1)
    a_other, b_other = jnp.stack(ring(other[:, :half], "rz")), jnp.stack(ring(other[:, half:], "fx"))
    a_other, b_other, a_near, b_near = tie((a_other, b_other, a_near, b_near))
    parts = []
    for own, other, near, axis, first in (
        (a_own, a_other, a_near, "fx", 0),
        (b_own, b_other, b_near, "rz", half),
    ):
        before, after = shift(other, axis, 1), shift(other, axis, -1)
        for value, y, far in (
            (own, 0, 0),
            (other, 1, 0),
            (near[0], 0, -1),
            (near[1], 0, 1),
            (before, 1, -1),
            (after, 1, 1),
            (shift(near[0], axis, 1), 0, 2),
            (shift(after, axis, -1), 1, 2),
        ):
            parts.append((value, first, [(d, y, far) if axis == "fx" else (far, y, d) for d in STEPS]))
    return parts


def reduce_rows(keep_a, keep_b, send_a, send_b):
    send_a, got_b = tie((send_a, swap(send_b, "cc")))
    got_a = swap(send_a, "cc")
    b = swap(low(total(keep_b[1], got_b[1])), "cy")
    a = [shift(low(total(keep_a[d], got_a[d])), "fx", d) for d in (1, 2, 3)]
    b_here = [low(total(keep_b[0, d], got_b[0, d], b[d])) for d in (1, 2, 3)]
    b_got = [shift(v, "fx", d) for v, d in zip(b_here, (1, 2, 3))]
    a_here = total(keep_a[0], got_a[0], *a)
    a_got = swap(low(a_here[1]), "cy")
    a_sum = a_here[0] + a_got.astype(jnp.float32)
    b_sum = total(keep_b[0, 0], got_b[0, 0], b[0], *b_got)
    return jnp.concatenate([low(a_sum), low(b_sum)], axis=0)


def body(features, tiles, tile_row, tile_col, tile_count, weight, bias):
    node_dev = features.shape[0] // lax.axis_size("fx")
    slots, side = tiles.shape[2], tiles.shape[3]
    place = [lax.axis_index(n) for n in NAMES]
    info = jnp.stack([tile_count.reshape(())] + [i.astype(jnp.int32) for i in place])
    parts = aggregate(
        tiles.reshape(slots, side, side),
        tile_row.reshape(slots),
        tile_col.reshape(slots),
        info,
        gather_sources(features.T),
        node_dev,
    )
    agg = reduce_rows(*parts)
    hidden = jnp.dot(agg, weight, preferred_element_type=jnp.float32) + bias
    return jax.nn.relu(hidden).astype(jnp.bfloat16)


def solution(mesh):
    fine = Mesh(mesh.devices.reshape(4, 2, 2, 2, 4), NAMES)
    row, col = ("rz", "ry"), ("cy", "cc")
    placed = (
        P(row + col, "fx"),
        P(row, col, "fx", None, None),
        P(row, col, "fx"),
        P(row, col, "fx"),
        P(row, col, "fx"),
        P(),
        P(),
    )
    return jax.shard_map(
        body, mesh=fine, in_specs=placed, out_specs=P(NAMES, None), check_vma=False
    )
```

```python
import functools

import jax
import jax.numpy as jnp
from jax import lax
from jax.experimental import pallas as pl
from jax.experimental.pallas import tpu as pltpu
from jax.sharding import Mesh
from jax.sharding import PartitionSpec as P

LOAD = 32
STEPS_AT_ONCE = (16, 4, 1)
PACK = 256
FIRST_X = 1024
NT = (((1,), (1,)), ((), ()))
NAMES = ("rz", "ry", "cy", "cc", "fx")


def aggregate_kernel(where, n_parts, rows_ref, cols_ref, info_ref, tiles_hbm, *refs):
    parts, (keep_a, keep_b, send_a, send_b) = refs[:n_parts], refs[n_parts : n_parts + 4]
    tiles, src, acc, stage, tile_sem, src_sem, out_sem = refs[n_parts + 4 :]
    side = tiles.shape[-1]
    per_row = src.shape[-1] // side
    count, rz, ry, cy, cc, fx = (info_ref[i] for i in range(6))
    loads = (count + LOAD - 1) // LOAD

    def tile_copy(i):
        part = pl.ds(pl.multiple_of(i * LOAD, LOAD), LOAD)
        return pltpu.make_async_copy(tiles_hbm.at[part], tiles.at[part], tile_sem.at[i])

    src_copies = []
    for ref, (first, offsets) in zip(parts, where):
        for n, (z, y, x) in enumerate(offsets):
            row = jnp.bitwise_and(rz + z, 3) * 2 + jnp.bitwise_xor(ry, y)
            col = jnp.bitwise_and(fx + x, 3)
            to = src.at[row, col, :, pl.ds(first, ref.shape[-1])]
            src_copies.append(pltpu.make_async_copy(ref.at[n], to, src_sem.at[len(src_copies)]))
    for copy in src_copies:
        copy.start()

    @pl.loop(0, loads)
    def _(i):
        tile_copy(i).start()

    zero_rows = 1024
    zeros = jnp.zeros((zero_rows, side), jnp.float32)

    @pl.loop(0, acc.shape[0] // zero_rows)
    def _(i):
        acc[pl.ds(pl.multiple_of(i * zero_rows, zero_rows), zero_rows), :] = zeros

    for copy in src_copies:
        copy.wait()

    def product(k):
        col = cols_ref[k]
        group = col // per_row
        lane = pl.multiple_of((col % per_row) * side, side)
        block = src[group, :, :, pl.ds(lane, side)].reshape(side, side)
        return lax.dot_general(tiles[k], block, NT, preferred_element_type=jnp.float32)

    def add(k, value):
        at = pl.ds(pl.multiple_of(rows_ref[k] * side, side), side)
        acc[at, :] += value

    @pl.loop(0, loads)
    def _(i):
        tile_copy(i).wait()
        first = i * LOAD
        here = jnp.minimum(count - first, LOAD)
        start = 0
        for width in STEPS_AT_ONCE:
            turns = (here - start) // width

            @pl.loop(0, turns)
            def _(s, start=start, width=width):
                k = first + start + s * width
                values = [product(k + t) for t in range(width)]
                for t in range(width):
                    add(k + t, values[t])

            start = start + turns * width

    slots, chunk = stage.shape[0], stage.shape[1]
    copies = []
    for n in range(16):
        other, y, d = n < 8, 1 - (n // 4) % 2, n % 4
        slot = n % slots
        if n >= slots:
            for copy in copies[n - slots]:
                copy.wait()
        core = 1 - cc if other else cc
        shard = (jnp.bitwise_xor(cy, y) * 2 + core) * 4 + jnp.bitwise_and(fx + d, 3)

        @pl.loop(0, chunk // PACK)
        def _(i, slot=slot, shard=shard):
            at = pl.multiple_of(i * PACK, PACK)
            rows = pl.ds(pl.multiple_of(shard * chunk + at, PACK), PACK)
            stage[slot, pl.ds(at, PACK), :] = acc[rows, :].astype(jnp.bfloat16)

        out_a, out_b = (send_a, send_b) if other else (keep_a, keep_b)
        copies.append(
            [
                pltpu.make_async_copy(
                    stage.at[slot, pl.ds(0, FIRST_X)], out_a.at[d, y], out_sem.at[slot, 0]
                ),
                pltpu.make_async_copy(
                    stage.at[slot, pl.ds(FIRST_X, chunk - FIRST_X)], out_b.at[y, d], out_sem.at[slot, 1]
                ),
            ]
        )
        for copy in copies[n]:
            copy.start()
    for n in range(16 - slots, 16):
        for copy in copies[n]:
            copy.wait()


def aggregate(tiles, rows, cols, info, parts, node_dev):
    slots, side, _ = tiles.shape
    any_space = pl.BlockSpec(memory_space=pl.ANY)
    arrays, where = [p[0] for p in parts], [p[1:] for p in parts]
    part_a = jax.ShapeDtypeStruct((4, 2, FIRST_X, side), jnp.bfloat16)
    part_b = jax.ShapeDtypeStruct((2, 4, node_dev - FIRST_X, side), jnp.bfloat16)
    return pl.pallas_call(
        functools.partial(aggregate_kernel, where, len(arrays)),
        out_shape=(part_a, part_b, part_a, part_b),
        grid_spec=pltpu.PrefetchScalarGridSpec(
            num_scalar_prefetch=3,
            grid=(1,),
            in_specs=[any_space] * (1 + len(arrays)),
            out_specs=(any_space,) * 4,
            scratch_shapes=[
                pltpu.VMEM(tiles.shape, jnp.bfloat16),
                pltpu.VMEM((8, 4, side // 4, 4 * node_dev), jnp.bfloat16),
                pltpu.VMEM((16 * node_dev, side), jnp.float32),
                pltpu.VMEM((4, node_dev, side), jnp.bfloat16),
                pltpu.SemaphoreType.DMA((slots // LOAD,)),
                pltpu.SemaphoreType.DMA((sum(len(w[1]) for w in where),)),
                pltpu.SemaphoreType.DMA((4, 2)),
            ],
        ),
        compiler_params=pltpu.CompilerParams(vmem_limit_bytes=56 * 2**20),
        name="aggregate",
    )(rows, cols, info, tiles, *arrays)


tie = lax.optimization_barrier


def swap(value, axis):
    return lax.ppermute(value, axis, [(0, 1), (1, 0)])


def shift(value, axis, by):
    n = lax.axis_size(axis)
    return lax.ppermute(value, axis, [(i, (i + by) % n) for i in range(n)])


def total(*values):
    wide = values[0].astype(jnp.float32)
    for value in values[1:]:
        wide = wide + value.astype(jnp.float32)
    return wide


def low(value):
    return value.astype(jnp.bfloat16)


STEPS = (0, 1, -1, 2)


def ring(value, axis):
    after, before = (shift(value, axis, -d) for d in STEPS[1:3])
    again, after, before = tie((value, after, before))
    return jnp.stack([value, after, before, shift(again, axis, 2)])


def ring_of_other(value, axis, own):
    return jnp.concatenate([jnp.stack([value, shift(value, axis, -1)]), swap(own[2:], "ry")])


def gather_sources(x):
    half = x.shape[1] // 2
    other = swap(x, "ry")
    a_own, b_own = ring(x[:, :half], "rz"), ring(x[:, half:], "fx")
    a_own, b_own = tie((a_own, b_own))
    a_near = shift(a_own, "fx", 1), shift(a_own, "fx", -1)
    b_near = shift(b_own, "rz", 1), shift(b_own, "rz", -1)
    a_other = ring_of_other(other[:, :half], "rz", a_own)
    b_other = ring_of_other(other[:, half:], "fx", b_own)
    a_other, b_other, a_near, b_near = tie((a_other, b_other, a_near, b_near))
    parts = []
    for own, other, near, axis, first in (
        (a_own, a_other, a_near, "fx", 0),
        (b_own, b_other, b_near, "rz", half),
    ):
        before, after = shift(other, axis, 1), shift(other, axis, -1)
        for value, y, far in (
            (own, 0, 0),
            (other, 1, 0),
            (near[0], 0, -1),
            (near[1], 0, 1),
            (before, 1, -1),
            (after, 1, 1),
            (shift(near[0], axis, 1), 0, 2),
            (shift(after, axis, -1), 1, 2),
        ):
            parts.append((value, first, [(d, y, far) if axis == "fx" else (far, y, d) for d in STEPS]))
    return parts


def reduce_rows(keep_a, keep_b, send_a, send_b):
    send_a, got_b = tie((send_a, swap(send_b, "cc")))
    got_a = swap(send_a, "cc")
    b = swap(low(total(keep_b[1], got_b[1])), "cy")
    a = [shift(low(total(keep_a[d], got_a[d])), "fx", d) for d in (1, 2, 3)]
    b_here = [low(total(keep_b[0, d], got_b[0, d], b[d])) for d in (1, 2, 3)]
    b_got = [shift(v, "fx", d) for v, d in zip(b_here, (1, 2, 3))]
    a_here = total(keep_a[0], got_a[0], *a)
    a_got = swap(low(a_here[1]), "cy")
    a_sum = a_here[0] + a_got.astype(jnp.float32)
    b_sum = total(keep_b[0, 0], got_b[0, 0], b[0], *b_got)
    return jnp.concatenate([low(a_sum), low(b_sum)], axis=0)


def body(features, tiles, tile_row, tile_col, tile_count, weight, bias):
    node_dev = features.shape[0] // lax.axis_size("fx")
    slots, side = tiles.shape[2], tiles.shape[3]
    place = [lax.axis_index(n) for n in NAMES]
    info = jnp.stack([tile_count.reshape(())] + [i.astype(jnp.int32) for i in place])
    parts = aggregate(
        tiles.reshape(slots, side, side),
        tile_row.reshape(slots),
        tile_col.reshape(slots),
        info,
        gather_sources(features.T),
        node_dev,
    )
    agg = reduce_rows(*parts)
    hidden = jnp.dot(agg, weight, preferred_element_type=jnp.float32) + bias
    return jax.nn.relu(hidden).astype(jnp.bfloat16)


def solution(mesh):
    fine = Mesh(mesh.devices.reshape(4, 2, 2, 2, 4), NAMES)
    row, col = ("rz", "ry"), ("cy", "cc")
    placed = (
        P(row + col, "fx"),
        P(row, col, "fx", None, None),
        P(row, col, "fx"),
        P(row, col, "fx"),
        P(row, col, "fx"),
        P(),
        P(),
    )
    return jax.shard_map(
        body, mesh=fine, in_specs=placed, out_specs=P(NAMES, None), check_vma=False
    )
```

```python
import functools

import jax
import jax.numpy as jnp
from jax import lax
from jax.experimental import pallas as pl
from jax.experimental.pallas import tpu as pltpu
from jax.sharding import Mesh
from jax.sharding import PartitionSpec as P

LOAD = 32
STEPS_AT_ONCE = (16, 4, 1)
PACK = 256
FIRST_X = 1024
NT = (((1,), (1,)), ((), ()))
NAMES = ("rz", "ry", "cy", "cc", "fx")


def aggregate_kernel(where, n_parts, rows_ref, cols_ref, info_ref, tiles_hbm, *refs):
    parts, (keep_a, keep_b, send_a, send_b) = refs[:n_parts], refs[n_parts : n_parts + 4]
    tiles, src, acc, stage, tile_sem, src_sem, out_sem = refs[n_parts + 4 :]
    side = tiles.shape[-1]
    per_row = src.shape[-1] // side
    count, rz, ry, cy, cc, fx = (info_ref[i] for i in range(6))
    loads = (count + LOAD - 1) // LOAD

    def tile_copy(i):
        part = pl.ds(pl.multiple_of(i * LOAD, LOAD), LOAD)
        return pltpu.make_async_copy(tiles_hbm.at[part], tiles.at[part], tile_sem.at[i])

    src_copies = []
    for ref, (first, offsets) in zip(parts, where):
        for n, (z, y, x) in enumerate(offsets):
            row = jnp.bitwise_and(rz + z, 3) * 2 + jnp.bitwise_xor(ry, y)
            col = jnp.bitwise_and(fx + x, 3)
            to = src.at[row, col, :, pl.ds(first, ref.shape[-1])]
            src_copies.append(pltpu.make_async_copy(ref.at[n], to, src_sem.at[len(src_copies)]))
    for copy in src_copies:
        copy.start()

    @pl.loop(0, loads)
    def _(i):
        tile_copy(i).start()

    zero_rows = 1024
    zeros = jnp.zeros((zero_rows, side), jnp.float32)

    @pl.loop(0, acc.shape[0] // zero_rows)
    def _(i):
        acc[pl.ds(pl.multiple_of(i * zero_rows, zero_rows), zero_rows), :] = zeros

    for copy in src_copies:
        copy.wait()

    def product(k):
        col = cols_ref[k]
        group = col // per_row
        lane = pl.multiple_of((col % per_row) * side, side)
        block = src[group, :, :, pl.ds(lane, side)].reshape(side, side)
        return lax.dot_general(tiles[k], block, NT, preferred_element_type=jnp.float32)

    def add(k, value):
        at = pl.ds(pl.multiple_of(rows_ref[k] * side, side), side)
        acc[at, :] += value

    @pl.loop(0, loads)
    def _(i):
        tile_copy(i).wait()
        first = i * LOAD
        here = jnp.minimum(count - first, LOAD)
        start = 0
        for width in STEPS_AT_ONCE:
            turns = (here - start) // width

            @pl.loop(0, turns)
            def _(s, start=start, width=width):
                k = first + start + s * width
                values = [product(k + t) for t in range(width)]
                for t in range(width):
                    add(k + t, values[t])

            start = start + turns * width

    slots, chunk = stage.shape[0], stage.shape[1]
    copies = []
    for n in range(16):
        other, y, d = n < 8, 1 - (n // 4) % 2, n % 4
        slot = n % slots
        if n >= slots:
            for copy in copies[n - slots]:
                copy.wait()
        core = 1 - cc if other else cc
        shard = (jnp.bitwise_xor(cy, y) * 2 + core) * 4 + jnp.bitwise_and(fx + d, 3)

        @pl.loop(0, chunk // PACK)
        def _(i, slot=slot, shard=shard):
            at = pl.multiple_of(i * PACK, PACK)
            rows = pl.ds(pl.multiple_of(shard * chunk + at, PACK), PACK)
            stage[slot, pl.ds(at, PACK), :] = acc[rows, :].astype(jnp.bfloat16)

        out_a, out_b = (send_a, send_b) if other else (keep_a, keep_b)
        copies.append(
            [
                pltpu.make_async_copy(
                    stage.at[slot, pl.ds(0, FIRST_X)], out_a.at[d, y], out_sem.at[slot, 0]
                ),
                pltpu.make_async_copy(
                    stage.at[slot, pl.ds(FIRST_X, chunk - FIRST_X)], out_b.at[y, d], out_sem.at[slot, 1]
                ),
            ]
        )
        for copy in copies[n]:
            copy.start()
    for n in range(16 - slots, 16):
        for copy in copies[n]:
            copy.wait()


def aggregate(tiles, rows, cols, info, parts, node_dev):
    slots, side, _ = tiles.shape
    any_space = pl.BlockSpec(memory_space=pl.ANY)
    arrays, where = [p[0] for p in parts], [p[1:] for p in parts]
    part_a = jax.ShapeDtypeStruct((4, 2, FIRST_X, side), jnp.bfloat16)
    part_b = jax.ShapeDtypeStruct((2, 4, node_dev - FIRST_X, side), jnp.bfloat16)
    return pl.pallas_call(
        functools.partial(aggregate_kernel, where, len(arrays)),
        out_shape=(part_a, part_b, part_a, part_b),
        grid_spec=pltpu.PrefetchScalarGridSpec(
            num_scalar_prefetch=3,
            grid=(1,),
            in_specs=[any_space] * (1 + len(arrays)),
            out_specs=(any_space,) * 4,
            scratch_shapes=[
                pltpu.VMEM(tiles.shape, jnp.bfloat16),
                pltpu.VMEM((8, 4, side // 4, 4 * node_dev), jnp.bfloat16),
                pltpu.VMEM((16 * node_dev, side), jnp.float32),
                pltpu.VMEM((4, node_dev, side), jnp.bfloat16),
                pltpu.SemaphoreType.DMA((slots // LOAD,)),
                pltpu.SemaphoreType.DMA((sum(len(w[1]) for w in where),)),
                pltpu.SemaphoreType.DMA((4, 2)),
            ],
        ),
        compiler_params=pltpu.CompilerParams(vmem_limit_bytes=56 * 2**20),
        name="aggregate",
    )(rows, cols, info, tiles, *arrays)


tie = lax.optimization_barrier


def swap(value, axis):
    return lax.ppermute(value, axis, [(0, 1), (1, 0)])


def shift(value, axis, by):
    n = lax.axis_size(axis)
    return lax.ppermute(value, axis, [(i, (i + by) % n) for i in range(n)])


def total(*values):
    wide = values[0].astype(jnp.float32)
    for value in values[1:]:
        wide = wide + value.astype(jnp.float32)
    return wide


def low(value):
    return value.astype(jnp.bfloat16)


STEPS = (0, 1, -1, 2)


def ring(value, axis, ahead):
    after, before = (shift(value, axis, -d) for d in STEPS[1:3])
    again, after, before, ahead = tie((value, after, before, ahead))
    return jnp.stack([value, after, before, shift(again, axis, 2)]), ahead


def gather_sources(x):
    half = x.shape[1] // 2
    other = swap(x, "ry")
    a_own, other = ring(x[:, :half], "rz", other)
    b_own, other = ring(x[:, half:], "fx", other)
    a_next, b_next = shift(other[:, :half], "rz", -1), shift(other[:, half:], "fx", -1)
    a_own, b_own, a_next, b_next = tie((a_own, b_own, a_next, b_next))
    a_near = shift(a_own, "fx", 1), shift(a_own, "fx", -1)
    b_near = shift(b_own, "rz", 1), shift(b_own, "rz", -1)
    a_other = jnp.concatenate([jnp.stack([other[:, :half], a_next]), swap(a_own[2:], "ry")])
    b_other = jnp.concatenate([jnp.stack([other[:, half:], b_next]), swap(b_own[2:], "ry")])
    a_other, b_other, a_near, b_near = tie((a_other, b_other, a_near, b_near))
    parts = []
    for own, other, near, axis, first in (
        (a_own, a_other, a_near, "fx", 0),
        (b_own, b_other, b_near, "rz", half),
    ):
        before, after = shift(other, axis, 1), shift(other, axis, -1)
        for value, y, far in (
            (own, 0, 0),
            (other, 1, 0),
            (near[0], 0, -1),
            (near[1], 0, 1),
            (before, 1, -1),
            (after, 1, 1),
            (shift(near[0], axis, 1), 0, 2),
            (shift(after, axis, -1), 1, 2),
        ):
            parts.append((value, first, [(d, y, far) if axis == "fx" else (far, y, d) for d in STEPS]))
    return parts


def reduce_rows(keep_a, keep_b, send_a, send_b):
    send_a, got_b = tie((send_a, swap(send_b, "cc")))
    got_a = swap(send_a, "cc")
    b = swap(low(total(keep_b[1], got_b[1])), "cy")
    a = [shift(low(total(keep_a[d], got_a[d])), "fx", d) for d in (1, 2, 3)]
    b_here = [low(total(keep_b[0, d], got_b[0, d], b[d])) for d in (1, 2, 3)]
    b_got = [shift(v, "fx", d) for v, d in zip(b_here, (1, 2, 3))]
    a_here = total(keep_a[0], got_a[0], *a)
    a_got = swap(low(a_here[1]), "cy")
    a_sum = a_here[0] + a_got.astype(jnp.float32)
    b_sum = total(keep_b[0, 0], got_b[0, 0], b[0], *b_got)
    return jnp.concatenate([low(a_sum), low(b_sum)], axis=0)


def body(features, tiles, tile_row, tile_col, tile_count, weight, bias):
    node_dev = features.shape[0] // lax.axis_size("fx")
    slots, side = tiles.shape[2], tiles.shape[3]
    place = [lax.axis_index(n) for n in NAMES]
    info = jnp.stack([tile_count.reshape(())] + [i.astype(jnp.int32) for i in place])
    parts = aggregate(
        tiles.reshape(slots, side, side),
        tile_row.reshape(slots),
        tile_col.reshape(slots),
        info,
        gather_sources(features.T),
        node_dev,
    )
    agg = reduce_rows(*parts)
    hidden = jnp.dot(agg, weight, preferred_element_type=jnp.float32) + bias
    return jax.nn.relu(hidden).astype(jnp.bfloat16)


def solution(mesh):
    fine = Mesh(mesh.devices.reshape(4, 2, 2, 2, 4), NAMES)
    row, col = ("rz", "ry"), ("cy", "cc")
    placed = (
        P(row + col, "fx"),
        P(row, col, "fx", None, None),
        P(row, col, "fx"),
        P(row, col, "fx"),
        P(row, col, "fx"),
        P(),
        P(),
    )
    return jax.shard_map(
        body, mesh=fine, in_specs=placed, out_specs=P(NAMES, None), check_vma=False
    )
```

```python
import functools

import jax
import jax.numpy as jnp
from jax import lax
from jax.experimental import pallas as pl
from jax.experimental.pallas import tpu as pltpu
from jax.sharding import Mesh
from jax.sharding import PartitionSpec as P

LOAD = 32
STEPS_AT_ONCE = (16, 4, 1)
PACK = 256
SPLIT = 28
FIRST_X = 1024
NT = (((1,), (1,)), ((), ()))
NAMES = ("rz", "ry", "cy", "cc", "fx")


def aggregate_kernel(where, n_parts, rows_ref, cols_ref, info_ref, tiles_hbm, *refs):
    parts, (keep_a, keep_b, send_a, send_b) = refs[:n_parts], refs[n_parts : n_parts + 4]
    tiles, src, acc, stage, tile_sem, src_sem, out_sem = refs[n_parts + 4 :]
    side = tiles.shape[-1]
    per_row = src.shape[-1] // side
    count, rz, ry, cy, cc, fx = (info_ref[i] for i in range(6))
    loads = (count + LOAD - 1) // LOAD

    def tile_copy(i):
        part = pl.ds(pl.multiple_of(i * LOAD, LOAD), LOAD)
        return pltpu.make_async_copy(tiles_hbm.at[part], tiles.at[part], tile_sem.at[i])

    src_copies = []
    for ref, (first, offsets) in zip(parts, where):
        for n, (z, y, x) in enumerate(offsets):
            row = jnp.bitwise_and(rz + z, 3) * 2 + jnp.bitwise_xor(ry, y)
            col = jnp.bitwise_and(fx + x, 3)
            to = src.at[row, col, :, pl.ds(first, ref.shape[-1])]
            src_copies.append(pltpu.make_async_copy(ref.at[n], to, src_sem.at[len(src_copies)]))
    for copy in src_copies:
        copy.start()

    @pl.loop(0, loads)
    def _(i):
        tile_copy(i).start()

    zero_rows = 1024
    zeros = jnp.zeros((zero_rows, side), jnp.float32)

    @pl.loop(0, acc.shape[0] // zero_rows)
    def _(i):
        acc[pl.ds(pl.multiple_of(i * zero_rows, zero_rows), zero_rows), :] = zeros

    for copy in src_copies:
        copy.wait()

    def product(k):
        col = cols_ref[k]
        group = col // per_row
        lane = pl.multiple_of((col % per_row) * side, side)
        block = src[group, :, :, pl.ds(lane, side)].reshape(side, side)
        return lax.dot_general(tiles[k], block, NT, preferred_element_type=jnp.float32)

    def add(k, value):
        at = pl.ds(pl.multiple_of(rows_ref[k] * side, side), side)
        acc[at, :] += value

    @pl.loop(0, loads)
    def _(i):
        tile_copy(i).wait()
        first = i * LOAD
        here = jnp.minimum(count - first, LOAD)
        start = 0
        for width in STEPS_AT_ONCE:
            turns = (here - start) // width

            @pl.loop(0, turns)
            def _(s, start=start, width=width):
                k = first + start + s * width
                values = [product(k + t) for t in range(width)]
                for t in range(width):
                    add(k + t, values[t])

            start = start + turns * width

    slots, chunk = stage.shape[0], stage.shape[1]
    copies = []
    for n in range(16):
        other, y, d = n < 8, 1 - (n // 4) % 2, n % 4
        slot = n % slots
        if n >= slots:
            for copy in copies[n - slots]:
                copy.wait()
        core = 1 - cc if other else cc
        shard = (jnp.bitwise_xor(cy, y) * 2 + core) * 4 + jnp.bitwise_and(fx + d, 3)

        @pl.loop(0, chunk // PACK)
        def _(i, slot=slot, shard=shard):
            at = pl.multiple_of(i * PACK, PACK)
            rows = pl.ds(pl.multiple_of(shard * chunk + at, PACK), PACK)
            stage[slot, pl.ds(at, PACK), :] = acc[rows, :].astype(jnp.bfloat16)

        out_a, out_b = (send_a, send_b) if other else (keep_a, keep_b)
        copies.append(
            [
                pltpu.make_async_copy(
                    stage.at[slot, pl.ds(0, FIRST_X)], out_a.at[d, y], out_sem.at[slot, 0]
                ),
                pltpu.make_async_copy(
                    stage.at[slot, pl.ds(FIRST_X, chunk - FIRST_X)], out_b.at[y, d], out_sem.at[slot, 1]
                ),
            ]
        )
        for copy in copies[n]:
            copy.start()
    for n in range(16 - slots, 16):
        for copy in copies[n]:
            copy.wait()


def aggregate(tiles, rows, cols, info, parts, node_dev):
    slots, side, _ = tiles.shape
    any_space = pl.BlockSpec(memory_space=pl.ANY)
    arrays, where = [p[0] for p in parts], [p[1:] for p in parts]
    part_a = jax.ShapeDtypeStruct((4, 2, FIRST_X, side), jnp.bfloat16)
    part_b = jax.ShapeDtypeStruct((2, 4, node_dev - FIRST_X, side), jnp.bfloat16)
    return pl.pallas_call(
        functools.partial(aggregate_kernel, where, len(arrays)),
        out_shape=(part_a, part_b, part_a, part_b),
        grid_spec=pltpu.PrefetchScalarGridSpec(
            num_scalar_prefetch=3,
            grid=(1,),
            in_specs=[any_space] * (1 + len(arrays)),
            out_specs=(any_space,) * 4,
            scratch_shapes=[
                pltpu.VMEM(tiles.shape, jnp.bfloat16),
                pltpu.VMEM((8, 4, side // 4, 4 * node_dev), jnp.bfloat16),
                pltpu.VMEM((16 * node_dev, side), jnp.float32),
                pltpu.VMEM((4, node_dev, side), jnp.bfloat16),
                pltpu.SemaphoreType.DMA((slots // LOAD,)),
                pltpu.SemaphoreType.DMA((sum(len(w[1]) for w in where),)),
                pltpu.SemaphoreType.DMA((4, 2)),
            ],
        ),
        compiler_params=pltpu.CompilerParams(vmem_limit_bytes=56 * 2**20),
        name="aggregate",
    )(rows, cols, info, tiles, *arrays)


tie = lax.optimization_barrier


def swap(value, axis):
    return lax.ppermute(value, axis, [(0, 1), (1, 0)])


def shift(value, axis, by):
    n = lax.axis_size(axis)
    return lax.ppermute(value, axis, [(i, (i + by) % n) for i in range(n)])


def total(*values):
    wide = values[0].astype(jnp.float32)
    for value in values[1:]:
        wide = wide + value.astype(jnp.float32)
    return wide


def low(value):
    return value.astype(jnp.bfloat16)


STEPS = (0, 1, -1, 2)


def ring(value, axis):
    after, before = (shift(value, axis, -d) for d in STEPS[1:3])
    again, after, before = tie((value, after, before))
    return jnp.stack([value, after, before, shift(again, axis, 2)])


def gather_sources(x):
    half = SPLIT * 128
    other = swap(x, "ry")
    a_own, b_own = ring(x[:, :half], "rz"), ring(x[:, half:], "fx")
    a_own, b_own = tie((a_own, b_own))
    a_near = shift(a_own, "fx", 1), shift(a_own, "fx", -1)
    b_near = shift(b_own, "rz", 1), shift(b_own, "rz", -1)
    a_cross, b_half = tie((swap(a_own[2:], "ry"), b_own[2:]))
    b_cross = swap(b_half, "ry")
    a_other = jnp.concatenate([jnp.stack([other[:, :half], shift(other[:, :half], "rz", -1)]), a_cross])
    b_other = jnp.concatenate([jnp.stack([other[:, half:], shift(other[:, half:], "fx", -1)]), b_cross])
    a_other, b_other, a_near, b_near = tie((a_other, b_other, a_near, b_near))
    a_before, a_after = shift(a_other, "fx", 1), shift(a_other, "fx", -1)
    b_before, b_after = swap(b_near[0], "ry"), shift(b_other, "rz", -1)
    parts = []
    for value, y, far in (
        (a_own, 0, 0),
        (a_other, 1, 0),
        (a_near[0], 0, -1),
        (a_near[1], 0, 1),
        (a_before, 1, -1),
        (a_after, 1, 1),
        (shift(a_near[0], "fx", 1), 0, 2),
        (shift(a_after, "fx", -1), 1, 2),
    ):
        parts.append((value, 0, [(d, y, far) for d in STEPS]))
    for value, y, far, near in (
        (b_own, 0, 0, STEPS),
        (b_other, 1, 0, STEPS),
        (b_near[0], 0, -1, STEPS),
        (b_near[1], 0, 1, STEPS),
        (b_before, 1, -1, STEPS),
        (b_after, 1, 1, STEPS),
        (shift(b_near[0], "rz", 1), 0, 2, STEPS),
        (shift(b_before[:2], "rz", 1), 1, 2, STEPS[:2]),
        (shift(b_after[2:], "rz", -1), 1, 2, STEPS[2:]),
    ):
        parts.append((value, half, [(far, y, d) for d in near]))
    return parts


def reduce_rows(keep_a, keep_b, send_a, send_b):
    send_a, got_b = tie((send_a, swap(send_b, "cc")))
    got_a = swap(send_a, "cc")
    b = swap(low(total(keep_b[1], got_b[1])), "cy")
    a = [shift(low(total(keep_a[d], got_a[d])), "fx", d) for d in (1, 2, 3)]
    b_here = [low(total(keep_b[0, d], got_b[0, d], b[d])) for d in (1, 2, 3)]
    b_got = [shift(v, "fx", d) for v, d in zip(b_here, (1, 2, 3))]
    a_here = total(keep_a[0], got_a[0], *a)
    a_got = swap(low(a_here[1]), "cy")
    a_sum = a_here[0] + a_got.astype(jnp.float32)
    b_sum = total(keep_b[0, 0], got_b[0, 0], b[0], *b_got)
    return jnp.concatenate([low(a_sum), low(b_sum)], axis=0)


def body(features, tiles, tile_row, tile_col, tile_count, weight, bias):
    node_dev = features.shape[0] // lax.axis_size("fx")
    slots, side = tiles.shape[2], tiles.shape[3]
    place = [lax.axis_index(n) for n in NAMES]
    info = jnp.stack([tile_count.reshape(())] + [i.astype(jnp.int32) for i in place])
    parts = aggregate(
        tiles.reshape(slots, side, side),
        tile_row.reshape(slots),
        tile_col.reshape(slots),
        info,
        gather_sources(features.T),
        node_dev,
    )
    agg = reduce_rows(*parts)
    hidden = jnp.dot(agg, weight, preferred_element_type=jnp.float32) + bias
    return jax.nn.relu(hidden).astype(jnp.bfloat16)


def solution(mesh):
    fine = Mesh(mesh.devices.reshape(4, 2, 2, 2, 4), NAMES)
    row, col = ("rz", "ry"), ("cy", "cc")
    placed = (
        P(row + col, "fx"),
        P(row, col, "fx", None, None),
        P(row, col, "fx"),
        P(row, col, "fx"),
        P(row, col, "fx"),
        P(),
        P(),
    )
    return jax.shard_map(
        body, mesh=fine, in_specs=placed, out_specs=P(NAMES, None), check_vma=False
    )
```

```python
import functools

import jax
import jax.numpy as jnp
from jax import lax
from jax.experimental import pallas as pl
from jax.experimental.pallas import tpu as pltpu
from jax.sharding import Mesh
from jax.sharding import PartitionSpec as P

LOAD = 32
STEPS_AT_ONCE = (16, 4, 1)
PACK = 256
SPLIT = 28
FIRST_X = 1024
NT = (((1,), (1,)), ((), ()))
NAMES = ("rz", "ry", "cy", "cc", "fx")


def aggregate_kernel(where, n_parts, rows_ref, cols_ref, info_ref, tiles_hbm, *refs):
    parts, (keep_a, keep_b, send_a, send_b) = refs[:n_parts], refs[n_parts : n_parts + 4]
    tiles, src, acc, stage, tile_sem, src_sem, out_sem = refs[n_parts + 4 :]
    side = tiles.shape[-1]
    per_row = src.shape[-1] // side
    count, rz, ry, cy, cc, fx = (info_ref[i] for i in range(6))
    loads = (count + LOAD - 1) // LOAD

    def tile_copy(i):
        part = pl.ds(pl.multiple_of(i * LOAD, LOAD), LOAD)
        return pltpu.make_async_copy(tiles_hbm.at[part], tiles.at[part], tile_sem.at[i])

    src_copies = []
    for ref, (first, offsets) in zip(parts, where):
        for n, (z, y, x) in enumerate(offsets):
            row = jnp.bitwise_and(rz + z, 3) * 2 + jnp.bitwise_xor(ry, y)
            col = jnp.bitwise_and(fx + x, 3)
            to = src.at[row, col, :, pl.ds(first, ref.shape[-1])]
            src_copies.append(pltpu.make_async_copy(ref.at[n], to, src_sem.at[len(src_copies)]))
    for copy in src_copies:
        copy.start()

    @pl.loop(0, loads)
    def _(i):
        tile_copy(i).start()

    zero_rows = 1024
    zeros = jnp.zeros((zero_rows, side), jnp.float32)

    @pl.loop(0, acc.shape[0] // zero_rows)
    def _(i):
        acc[pl.ds(pl.multiple_of(i * zero_rows, zero_rows), zero_rows), :] = zeros

    for copy in src_copies:
        copy.wait()

    def product(k):
        col = cols_ref[k]
        group = col // per_row
        lane = pl.multiple_of((col % per_row) * side, side)
        block = src[group, :, :, pl.ds(lane, side)].reshape(side, side)
        return lax.dot_general(tiles[k], block, NT, preferred_element_type=jnp.float32)

    def add(k, value):
        at = pl.ds(pl.multiple_of(rows_ref[k] * side, side), side)
        acc[at, :] += value

    @pl.loop(0, loads)
    def _(i):
        tile_copy(i).wait()
        first = i * LOAD
        here = jnp.minimum(count - first, LOAD)
        start = 0
        for width in STEPS_AT_ONCE:
            turns = (here - start) // width

            @pl.loop(0, turns)
            def _(s, start=start, width=width):
                k = first + start + s * width
                values = [product(k + t) for t in range(width)]
                for t in range(width):
                    add(k + t, values[t])

            start = start + turns * width

    slots, chunk = stage.shape[0], stage.shape[1]
    copies = []
    for n in range(16):
        other, y, d = n < 8, 1 - (n // 4) % 2, n % 4
        slot = n % slots
        if n >= slots:
            for copy in copies[n - slots]:
                copy.wait()
        core = 1 - cc if other else cc
        shard = (jnp.bitwise_xor(cy, y) * 2 + core) * 4 + jnp.bitwise_and(fx + d, 3)

        @pl.loop(0, chunk // PACK)
        def _(i, slot=slot, shard=shard):
            at = pl.multiple_of(i * PACK, PACK)
            rows = pl.ds(pl.multiple_of(shard * chunk + at, PACK), PACK)
            stage[slot, pl.ds(at, PACK), :] = acc[rows, :].astype(jnp.bfloat16)

        out_a, out_b = (send_a, send_b) if other else (keep_a, keep_b)
        copies.append(
            [
                pltpu.make_async_copy(
                    stage.at[slot, pl.ds(0, FIRST_X)], out_a.at[d, y], out_sem.at[slot, 0]
                ),
                pltpu.make_async_copy(
                    stage.at[slot, pl.ds(FIRST_X, chunk - FIRST_X)], out_b.at[y, d], out_sem.at[slot, 1]
                ),
            ]
        )
        for copy in copies[n]:
            copy.start()
    for n in range(16 - slots, 16):
        for copy in copies[n]:
            copy.wait()


def aggregate(tiles, rows, cols, info, parts, node_dev):
    slots, side, _ = tiles.shape
    any_space = pl.BlockSpec(memory_space=pl.ANY)
    arrays, where = [p[0] for p in parts], [p[1:] for p in parts]
    part_a = jax.ShapeDtypeStruct((4, 2, FIRST_X, side), jnp.bfloat16)
    part_b = jax.ShapeDtypeStruct((2, 4, node_dev - FIRST_X, side), jnp.bfloat16)
    return pl.pallas_call(
        functools.partial(aggregate_kernel, where, len(arrays)),
        out_shape=(part_a, part_b, part_a, part_b),
        grid_spec=pltpu.PrefetchScalarGridSpec(
            num_scalar_prefetch=3,
            grid=(1,),
            in_specs=[any_space] * (1 + len(arrays)),
            out_specs=(any_space,) * 4,
            scratch_shapes=[
                pltpu.VMEM(tiles.shape, jnp.bfloat16),
                pltpu.VMEM((8, 4, side // 4, 4 * node_dev), jnp.bfloat16),
                pltpu.VMEM((16 * node_dev, side), jnp.float32),
                pltpu.VMEM((4, node_dev, side), jnp.bfloat16),
                pltpu.SemaphoreType.DMA((slots // LOAD,)),
                pltpu.SemaphoreType.DMA((sum(len(w[1]) for w in where),)),
                pltpu.SemaphoreType.DMA((4, 2)),
            ],
        ),
        compiler_params=pltpu.CompilerParams(vmem_limit_bytes=56 * 2**20),
        name="aggregate",
    )(rows, cols, info, tiles, *arrays)


tie = lax.optimization_barrier


def swap(value, axis):
    return lax.ppermute(value, axis, [(0, 1), (1, 0)])


def shift(value, axis, by):
    n = lax.axis_size(axis)
    return lax.ppermute(value, axis, [(i, (i + by) % n) for i in range(n)])


def total(*values):
    wide = values[0].astype(jnp.float32)
    for value in values[1:]:
        wide = wide + value.astype(jnp.float32)
    return wide


def low(value):
    return value.astype(jnp.bfloat16)


STEPS = (0, 1, -1, 2)


def ring(value, axis):
    after, before = (shift(value, axis, -d) for d in STEPS[1:3])
    again, after, before = tie((value, after, before))
    return jnp.stack([value, after, before, shift(again, axis, 2)])


def gather_sources(x):
    half = SPLIT * 128
    other = swap(x, "ry")
    a_own, b_own = ring(x[:, :half], "rz"), ring(x[:, half:], "fx")
    a_own, b_own = tie((a_own, b_own))
    a_near = shift(a_own, "fx", 1), shift(a_own, "fx", -1)
    b_near = shift(b_own, "rz", 1), shift(b_own, "rz", -1)
    a_other = jnp.concatenate(
        [jnp.stack([other[:, :half], shift(other[:, :half], "rz", -1)]), swap(a_own[2:], "ry")]
    )
    b_other = jnp.concatenate(
        [jnp.stack([other[:, half:], shift(other[:, half:], "fx", -1)]), swap(b_own[2:], "ry")]
    )
    a_other, b_other, a_near, b_near = tie((a_other, b_other, a_near, b_near))
    a_before, a_after = shift(a_other, "fx", 1), shift(a_other, "fx", -1)
    b_before, b_after = swap(b_near[0], "ry"), shift(b_other, "rz", -1)
    parts = []
    for value, y, far in (
        (a_own, 0, 0),
        (a_other, 1, 0),
        (a_near[0], 0, -1),
        (a_near[1], 0, 1),
        (a_before, 1, -1),
        (a_after, 1, 1),
        (shift(a_near[0], "fx", 1), 0, 2),
        (shift(a_after, "fx", -1), 1, 2),
    ):
        parts.append((value, 0, [(d, y, far) for d in STEPS]))
    for value, y, far, near in (
        (b_own, 0, 0, STEPS),
        (b_other, 1, 0, STEPS),
        (b_near[0], 0, -1, STEPS),
        (b_near[1], 0, 1, STEPS),
        (b_before, 1, -1, STEPS),
        (b_after, 1, 1, STEPS),
        (shift(b_near[0], "rz", 1), 0, 2, STEPS),
        (shift(b_before[:2], "rz", 1), 1, 2, STEPS[:2]),
        (shift(b_after[2:], "rz", -1), 1, 2, STEPS[2:]),
    ):
        parts.append((value, half, [(far, y, d) for d in near]))
    return parts


def reduce_rows(keep_a, keep_b, send_a, send_b):
    send_a, got_b = tie((send_a, swap(send_b, "cc")))
    got_a = swap(send_a, "cc")
    b = swap(low(total(keep_b[1], got_b[1])), "cy")
    a = [shift(low(total(keep_a[d], got_a[d])), "fx", d) for d in (1, 2, 3)]
    b_here = [low(total(keep_b[0, d], got_b[0, d], b[d])) for d in (1, 2, 3)]
    b_got = [shift(v, "fx", d) for v, d in zip(b_here, (1, 2, 3))]
    a_here = total(keep_a[0], got_a[0], *a)
    a_got = swap(low(a_here[1]), "cy")
    a_sum = a_here[0] + a_got.astype(jnp.float32)
    b_sum = total(keep_b[0, 0], got_b[0, 0], b[0], *b_got)
    return jnp.concatenate([low(a_sum), low(b_sum)], axis=0)


def body(features, tiles, tile_row, tile_col, tile_count, weight, bias):
    node_dev = features.shape[0] // lax.axis_size("fx")
    slots, side = tiles.shape[2], tiles.shape[3]
    place = [lax.axis_index(n) for n in NAMES]
    info = jnp.stack([tile_count.reshape(())] + [i.astype(jnp.int32) for i in place])
    parts = aggregate(
        tiles.reshape(slots, side, side),
        tile_row.reshape(slots),
        tile_col.reshape(slots),
        info,
        gather_sources(features.T),
        node_dev,
    )
    agg = reduce_rows(*parts)
    hidden = jnp.dot(agg, weight, preferred_element_type=jnp.float32) + bias
    return jax.nn.relu(hidden).astype(jnp.bfloat16)


def solution(mesh):
    fine = Mesh(mesh.devices.reshape(4, 2, 2, 2, 4), NAMES)
    row, col = ("rz", "ry"), ("cy", "cc")
    placed = (
        P(row + col, "fx"),
        P(row, col, "fx", None, None),
        P(row, col, "fx"),
        P(row, col, "fx"),
        P(row, col, "fx"),
        P(),
        P(),
    )
    return jax.shard_map(
        body, mesh=fine, in_specs=placed, out_specs=P(NAMES, None), check_vma=False
    )
```

```python
import functools

import jax
import jax.numpy as jnp
from jax import lax
from jax.experimental import pallas as pl
from jax.experimental.pallas import tpu as pltpu
from jax.sharding import Mesh
from jax.sharding import PartitionSpec as P

LOAD = 32
STEPS_AT_ONCE = (16, 4, 1)
PACK = 256
SPLIT = 28
FIRST_X = 1024
NT = (((1,), (1,)), ((), ()))
NAMES = ("rz", "ry", "cy", "cc", "fx")


def aggregate_kernel(where, n_parts, rows_ref, cols_ref, info_ref, tiles_hbm, *refs):
    parts, (keep_a, keep_b, send_a, send_b) = refs[:n_parts], refs[n_parts : n_parts + 4]
    tiles, src, acc, stage, tile_sem, src_sem, out_sem = refs[n_parts + 4 :]
    side = tiles.shape[-1]
    per_row = src.shape[-1] // side
    count, rz, ry, cy, cc, fx = (info_ref[i] for i in range(6))
    loads = (count + LOAD - 1) // LOAD

    def tile_copy(i):
        part = pl.ds(pl.multiple_of(i * LOAD, LOAD), LOAD)
        return pltpu.make_async_copy(tiles_hbm.at[part], tiles.at[part], tile_sem.at[i])

    src_copies = []
    for ref, (first, offsets) in zip(parts, where):
        for n, (z, y, x) in enumerate(offsets):
            row = jnp.bitwise_and(rz + z, 3) * 2 + jnp.bitwise_xor(ry, y)
            col = jnp.bitwise_and(fx + x, 3)
            to = src.at[row, col, :, pl.ds(first, ref.shape[-1])]
            src_copies.append(pltpu.make_async_copy(ref.at[n], to, src_sem.at[len(src_copies)]))
    for copy in src_copies:
        copy.start()

    @pl.loop(0, loads)
    def _(i):
        tile_copy(i).start()

    zero_rows = 1024
    zeros = jnp.zeros((zero_rows, side), jnp.float32)

    @pl.loop(0, acc.shape[0] // zero_rows)
    def _(i):
        acc[pl.ds(pl.multiple_of(i * zero_rows, zero_rows), zero_rows), :] = zeros

    for copy in src_copies:
        copy.wait()

    def product(k):
        col = cols_ref[k]
        group = col // per_row
        lane = pl.multiple_of((col % per_row) * side, side)
        block = src[group, :, :, pl.ds(lane, side)].reshape(side, side)
        return lax.dot_general(tiles[k], block, NT, preferred_element_type=jnp.float32)

    def add(k, value):
        at = pl.ds(pl.multiple_of(rows_ref[k] * side, side), side)
        acc[at, :] += value

    @pl.loop(0, loads)
    def _(i):
        tile_copy(i).wait()
        first = i * LOAD
        here = jnp.minimum(count - first, LOAD)
        start = 0
        for width in STEPS_AT_ONCE:
            turns = (here - start) // width

            @pl.loop(0, turns)
            def _(s, start=start, width=width):
                k = first + start + s * width
                values = [product(k + t) for t in range(width)]
                for t in range(width):
                    add(k + t, values[t])

            start = start + turns * width

    slots, chunk = stage.shape[0], stage.shape[1]
    copies = []
    for n in range(16):
        other, y, d = n < 8, 1 - (n // 4) % 2, n % 4
        slot = n % slots
        if n >= slots:
            for copy in copies[n - slots]:
                copy.wait()
        core = 1 - cc if other else cc
        shard = (jnp.bitwise_xor(cy, y) * 2 + core) * 4 + jnp.bitwise_and(fx + d, 3)

        @pl.loop(0, chunk // PACK)
        def _(i, slot=slot, shard=shard):
            at = pl.multiple_of(i * PACK, PACK)
            rows = pl.ds(pl.multiple_of(shard * chunk + at, PACK), PACK)
            stage[slot, pl.ds(at, PACK), :] = acc[rows, :].astype(jnp.bfloat16)

        out_a, out_b = (send_a, send_b) if other else (keep_a, keep_b)
        copies.append(
            [
                pltpu.make_async_copy(
                    stage.at[slot, pl.ds(0, FIRST_X)], out_a.at[d, y], out_sem.at[slot, 0]
                ),
                pltpu.make_async_copy(
                    stage.at[slot, pl.ds(FIRST_X, chunk - FIRST_X)], out_b.at[y, d], out_sem.at[slot, 1]
                ),
            ]
        )
        for copy in copies[n]:
            copy.start()
    for n in range(16 - slots, 16):
        for copy in copies[n]:
            copy.wait()


def aggregate(tiles, rows, cols, info, parts, node_dev):
    slots, side, _ = tiles.shape
    any_space = pl.BlockSpec(memory_space=pl.ANY)
    arrays, where = [p[0] for p in parts], [p[1:] for p in parts]
    part_a = jax.ShapeDtypeStruct((4, 2, FIRST_X, side), jnp.bfloat16)
    part_b = jax.ShapeDtypeStruct((2, 4, node_dev - FIRST_X, side), jnp.bfloat16)
    return pl.pallas_call(
        functools.partial(aggregate_kernel, where, len(arrays)),
        out_shape=(part_a, part_b, part_a, part_b),
        grid_spec=pltpu.PrefetchScalarGridSpec(
            num_scalar_prefetch=3,
            grid=(1,),
            in_specs=[any_space] * (1 + len(arrays)),
            out_specs=(any_space,) * 4,
            scratch_shapes=[
                pltpu.VMEM(tiles.shape, jnp.bfloat16),
                pltpu.VMEM((8, 4, side // 4, 4 * node_dev), jnp.bfloat16),
                pltpu.VMEM((16 * node_dev, side), jnp.float32),
                pltpu.VMEM((4, node_dev, side), jnp.bfloat16),
                pltpu.SemaphoreType.DMA((slots // LOAD,)),
                pltpu.SemaphoreType.DMA((sum(len(w[1]) for w in where),)),
                pltpu.SemaphoreType.DMA((4, 2)),
            ],
        ),
        compiler_params=pltpu.CompilerParams(vmem_limit_bytes=56 * 2**20),
        name="aggregate",
    )(rows, cols, info, tiles, *arrays)


tie = lax.optimization_barrier


def swap(value, axis):
    return lax.ppermute(value, axis, [(0, 1), (1, 0)])


def shift(value, axis, by):
    n = lax.axis_size(axis)
    return lax.ppermute(value, axis, [(i, (i + by) % n) for i in range(n)])


def total(*values):
    wide = values[0].astype(jnp.float32)
    for value in values[1:]:
        wide = wide + value.astype(jnp.float32)
    return wide


def low(value):
    return value.astype(jnp.bfloat16)


STEPS = (0, 1, -1, 2)


def rings(*pairs):
    near = tie([(value, *(shift(value, axis, -d) for d in STEPS[1:3])) for value, axis in pairs])
    return [jnp.stack([*three, shift(three[0], axis, 2)]) for three, (_, axis) in zip(near, pairs)]


def gather_sources(x):
    half = SPLIT * 128
    other = swap(x, "ry")
    a_own, b_own = rings((x[:, :half], "rz"), (x[:, half:], "fx"))
    a_own, b_own = tie((a_own, b_own))
    a_near = shift(a_own, "fx", 1), shift(a_own, "fx", -1)
    b_near = shift(b_own, "rz", 1), shift(b_own, "rz", -1)
    a_other = jnp.concatenate(
        [jnp.stack([other[:, :half], shift(other[:, :half], "rz", -1)]), swap(a_own[2:], "ry")]
    )
    b_other = jnp.concatenate(
        [jnp.stack([other[:, half:], shift(other[:, half:], "fx", -1)]), swap(b_own[2:], "ry")]
    )
    a_other, b_other, a_near, b_near = tie((a_other, b_other, a_near, b_near))
    a_before, a_after = shift(a_other, "fx", 1), shift(a_other, "fx", -1)
    b_before, b_after = swap(b_near[0], "ry"), shift(b_other, "rz", -1)
    parts = []
    for value, y, far in (
        (a_own, 0, 0),
        (a_other, 1, 0),
        (a_near[0], 0, -1),
        (a_near[1], 0, 1),
        (a_before, 1, -1),
        (a_after, 1, 1),
        (shift(a_near[0], "fx", 1), 0, 2),
        (shift(a_after, "fx", -1), 1, 2),
    ):
        parts.append((value, 0, [(d, y, far) for d in STEPS]))
    for value, y, far, near in (
        (b_own, 0, 0, STEPS),
        (b_other, 1, 0, STEPS),
        (b_near[0], 0, -1, STEPS),
        (b_near[1], 0, 1, STEPS),
        (b_before, 1, -1, STEPS),
        (b_after, 1, 1, STEPS),
        (shift(b_near[0], "rz", 1), 0, 2, STEPS),
        (shift(b_before[:2], "rz", 1), 1, 2, STEPS[:2]),
        (shift(b_after[2:], "rz", -1), 1, 2, STEPS[2:]),
    ):
        parts.append((value, half, [(far, y, d) for d in near]))
    return parts


def reduce_rows(keep_a, keep_b, send_a, send_b):
    send_a, got_b = tie((send_a, swap(send_b, "cc")))
    got_a = swap(send_a, "cc")
    b = swap(low(total(keep_b[1], got_b[1])), "cy")
    a = [shift(low(total(keep_a[d], got_a[d])), "fx", d) for d in (1, 2, 3)]
    b_here = [low(total(keep_b[0, d], got_b[0, d], b[d])) for d in (1, 2, 3)]
    b_got = [shift(v, "fx", d) for v, d in zip(b_here, (1, 2, 3))]
    a_here = total(keep_a[0], got_a[0], *a)
    a_got = swap(low(a_here[1]), "cy")
    a_sum = a_here[0] + a_got.astype(jnp.float32)
    b_sum = total(keep_b[0, 0], got_b[0, 0], b[0], *b_got)
    return jnp.concatenate([low(a_sum), low(b_sum)], axis=0)


def body(features, tiles, tile_row, tile_col, tile_count, weight, bias):
    node_dev = features.shape[0] // lax.axis_size("fx")
    slots, side = tiles.shape[2], tiles.shape[3]
    place = [lax.axis_index(n) for n in NAMES]
    info = jnp.stack([tile_count.reshape(())] + [i.astype(jnp.int32) for i in place])
    parts = aggregate(
        tiles.reshape(slots, side, side),
        tile_row.reshape(slots),
        tile_col.reshape(slots),
        info,
        gather_sources(features.T),
        node_dev,
    )
    agg = reduce_rows(*parts)
    hidden = jnp.dot(agg, weight, preferred_element_type=jnp.float32) + bias
    return jax.nn.relu(hidden).astype(jnp.bfloat16)


def solution(mesh):
    fine = Mesh(mesh.devices.reshape(4, 2, 2, 2, 4), NAMES)
    row, col = ("rz", "ry"), ("cy", "cc")
    placed = (
        P(row + col, "fx"),
        P(row, col, "fx", None, None),
        P(row, col, "fx"),
        P(row, col, "fx"),
        P(row, col, "fx"),
        P(),
        P(),
    )
    return jax.shard_map(
        body, mesh=fine, in_specs=placed, out_specs=P(NAMES, None), check_vma=False
    )
```

```python
import functools

import jax
import jax.numpy as jnp
from jax import lax
from jax.experimental import pallas as pl
from jax.experimental.pallas import tpu as pltpu
from jax.sharding import Mesh
from jax.sharding import PartitionSpec as P

LOAD = 32
STEPS_AT_ONCE = (32, 8, 1)
PACK = 256
SPLIT = 28
FIRST_X = 1024
NT = (((1,), (1,)), ((), ()))
NAMES = ("rz", "ry", "cy", "cc", "fx")


def aggregate_kernel(where, n_parts, rows_ref, cols_ref, info_ref, tiles_hbm, *refs):
    parts, (keep_a, keep_b, send_a, send_b) = refs[:n_parts], refs[n_parts : n_parts + 4]
    tiles, src, acc, stage, tile_sem, src_sem, out_sem = refs[n_parts + 4 :]
    side = tiles.shape[-1]
    per_row = src.shape[-1] // side
    count, rz, ry, cy, cc, fx = (info_ref[i] for i in range(6))
    loads = (count + LOAD - 1) // LOAD

    def tile_copy(i):
        part = pl.ds(pl.multiple_of(i * LOAD, LOAD), LOAD)
        return pltpu.make_async_copy(tiles_hbm.at[part], tiles.at[part], tile_sem.at[i])

    src_copies = []
    for ref, (first, offsets) in zip(parts, where):
        for n, (z, y, x) in enumerate(offsets):
            row = jnp.bitwise_and(rz + z, 3) * 2 + jnp.bitwise_xor(ry, y)
            col = jnp.bitwise_and(fx + x, 3)
            to = src.at[row, col, :, pl.ds(first, ref.shape[-1])]
            src_copies.append(pltpu.make_async_copy(ref.at[n], to, src_sem.at[len(src_copies)]))
    for copy in src_copies:
        copy.start()

    @pl.loop(0, loads)
    def _(i):
        tile_copy(i).start()

    zero_rows = 1024
    zeros = jnp.zeros((zero_rows, side), jnp.float32)

    @pl.loop(0, acc.shape[0] // zero_rows)
    def _(i):
        acc[pl.ds(pl.multiple_of(i * zero_rows, zero_rows), zero_rows), :] = zeros

    for copy in src_copies:
        copy.wait()

    def product(k):
        col = cols_ref[k]
        group = col // per_row
        lane = pl.multiple_of((col % per_row) * side, side)
        block = src[group, :, :, pl.ds(lane, side)].reshape(side, side)
        return lax.dot_general(tiles[k], block, NT, preferred_element_type=jnp.float32)

    def add(k, value):
        at = pl.ds(pl.multiple_of(rows_ref[k] * side, side), side)
        acc[at, :] += value

    @pl.loop(0, loads)
    def _(i):
        tile_copy(i).wait()
        first = i * LOAD
        here = jnp.minimum(count - first, LOAD)
        start = 0
        for width in STEPS_AT_ONCE:
            turns = (here - start) // width

            @pl.loop(0, turns)
            def _(s, start=start, width=width):
                k = first + start + s * width
                values = [product(k + t) for t in range(width)]
                for t in range(width):
                    add(k + t, values[t])

            start = start + turns * width

    slots, chunk = stage.shape[0], stage.shape[1]
    copies = []
    for n in range(16):
        other, y, d = n < 8, 1 - (n // 4) % 2, n % 4
        slot = n % slots
        if n >= slots:
            for copy in copies[n - slots]:
                copy.wait()
        core = 1 - cc if other else cc
        shard = (jnp.bitwise_xor(cy, y) * 2 + core) * 4 + jnp.bitwise_and(fx + d, 3)

        @pl.loop(0, chunk // PACK)
        def _(i, slot=slot, shard=shard):
            at = pl.multiple_of(i * PACK, PACK)
            rows = pl.ds(pl.multiple_of(shard * chunk + at, PACK), PACK)
            stage[slot, pl.ds(at, PACK), :] = acc[rows, :].astype(jnp.bfloat16)

        out_a, out_b = (send_a, send_b) if other else (keep_a, keep_b)
        copies.append(
            [
                pltpu.make_async_copy(
                    stage.at[slot, pl.ds(0, FIRST_X)], out_a.at[d, y], out_sem.at[slot, 0]
                ),
                pltpu.make_async_copy(
                    stage.at[slot, pl.ds(FIRST_X, chunk - FIRST_X)], out_b.at[y, d], out_sem.at[slot, 1]
                ),
            ]
        )
        for copy in copies[n]:
            copy.start()
    for n in range(16 - slots, 16):
        for copy in copies[n]:
            copy.wait()


def aggregate(tiles, rows, cols, info, parts, node_dev):
    slots, side, _ = tiles.shape
    any_space = pl.BlockSpec(memory_space=pl.ANY)
    arrays, where = [p[0] for p in parts], [p[1:] for p in parts]
    part_a = jax.ShapeDtypeStruct((4, 2, FIRST_X, side), jnp.bfloat16)
    part_b = jax.ShapeDtypeStruct((2, 4, node_dev - FIRST_X, side), jnp.bfloat16)
    return pl.pallas_call(
        functools.partial(aggregate_kernel, where, len(arrays)),
        out_shape=(part_a, part_b, part_a, part_b),
        grid_spec=pltpu.PrefetchScalarGridSpec(
            num_scalar_prefetch=3,
            grid=(1,),
            in_specs=[any_space] * (1 + len(arrays)),
            out_specs=(any_space,) * 4,
            scratch_shapes=[
                pltpu.VMEM(tiles.shape, jnp.bfloat16),
                pltpu.VMEM((8, 4, side // 4, 4 * node_dev), jnp.bfloat16),
                pltpu.VMEM((16 * node_dev, side), jnp.float32),
                pltpu.VMEM((4, node_dev, side), jnp.bfloat16),
                pltpu.SemaphoreType.DMA((slots // LOAD,)),
                pltpu.SemaphoreType.DMA((sum(len(w[1]) for w in where),)),
                pltpu.SemaphoreType.DMA((4, 2)),
            ],
        ),
        compiler_params=pltpu.CompilerParams(vmem_limit_bytes=56 * 2**20),
        name="aggregate",
    )(rows, cols, info, tiles, *arrays)


tie = lax.optimization_barrier


def swap(value, axis):
    return lax.ppermute(value, axis, [(0, 1), (1, 0)])


def shift(value, axis, by):
    n = lax.axis_size(axis)
    return lax.ppermute(value, axis, [(i, (i + by) % n) for i in range(n)])


def total(*values):
    wide = values[0].astype(jnp.float32)
    for value in values[1:]:
        wide = wide + value.astype(jnp.float32)
    return wide


def low(value):
    return value.astype(jnp.bfloat16)


STEPS = (0, 1, -1, 2)


def rings(*pairs):
    near = tie([(value, *(shift(value, axis, -d) for d in STEPS[1:3])) for value, axis in pairs])
    return [jnp.stack([*three, shift(three[0], axis, 2)]) for three, (_, axis) in zip(near, pairs)]


def gather_sources(x):
    half = SPLIT * 128
    other = swap(x, "ry")
    a_own, b_own = rings((x[:, :half], "rz"), (x[:, half:], "fx"))
    a_own, b_own = tie((a_own, b_own))
    a_near = shift(a_own, "fx", 1), shift(a_own, "fx", -1)
    b_near = shift(b_own, "rz", 1), shift(b_own, "rz", -1)
    a_other = jnp.concatenate(
        [jnp.stack([other[:, :half], shift(other[:, :half], "rz", -1)]), swap(a_own[2:], "ry")]
    )
    b_other = jnp.concatenate(
        [jnp.stack([other[:, half:], shift(other[:, half:], "fx", -1)]), swap(b_own[2:], "ry")]
    )
    a_other, b_other, a_near, b_near = tie((a_other, b_other, a_near, b_near))
    a_before, a_after = shift(a_other, "fx", 1), shift(a_other, "fx", -1)
    b_before, b_after = swap(b_near[0], "ry"), shift(b_other, "rz", -1)
    parts = []
    for value, y, far in (
        (a_own, 0, 0),
        (a_other, 1, 0),
        (a_near[0], 0, -1),
        (a_near[1], 0, 1),
        (a_before, 1, -1),
        (a_after, 1, 1),
        (shift(a_near[0], "fx", 1), 0, 2),
        (shift(a_after, "fx", -1), 1, 2),
    ):
        parts.append((value, 0, [(d, y, far) for d in STEPS]))
    for value, y, far, near in (
        (b_own, 0, 0, STEPS),
        (b_other, 1, 0, STEPS),
        (b_near[0], 0, -1, STEPS),
        (b_near[1], 0, 1, STEPS),
        (b_before, 1, -1, STEPS),
        (b_after, 1, 1, STEPS),
        (shift(b_near[0], "rz", 1), 0, 2, STEPS),
        (shift(b_before[:2], "rz", 1), 1, 2, STEPS[:2]),
        (shift(b_after[2:], "rz", -1), 1, 2, STEPS[2:]),
    ):
        parts.append((value, half, [(far, y, d) for d in near]))
    return parts


def reduce_rows(keep_a, keep_b, send_a, send_b):
    send_a, got_b = tie((send_a, swap(send_b, "cc")))
    got_a = swap(send_a, "cc")
    b = swap(low(total(keep_b[1], got_b[1])), "cy")
    a = [shift(low(total(keep_a[d], got_a[d])), "fx", d) for d in (1, 2, 3)]
    b_here = [low(total(keep_b[0, d], got_b[0, d], b[d])) for d in (1, 2, 3)]
    b_got = [shift(v, "fx", d) for v, d in zip(b_here, (1, 2, 3))]
    a_here = total(keep_a[0], got_a[0], *a)
    a_got = swap(low(a_here[1]), "cy")
    a_sum = a_here[0] + a_got.astype(jnp.float32)
    b_sum = total(keep_b[0, 0], got_b[0, 0], b[0], *b_got)
    return jnp.concatenate([low(a_sum), low(b_sum)], axis=0)


def body(features, tiles, tile_row, tile_col, tile_count, weight, bias):
    node_dev = features.shape[0] // lax.axis_size("fx")
    slots, side = tiles.shape[2], tiles.shape[3]
    place = [lax.axis_index(n) for n in NAMES]
    info = jnp.stack([tile_count.reshape(())] + [i.astype(jnp.int32) for i in place])
    parts = aggregate(
        tiles.reshape(slots, side, side),
        tile_row.reshape(slots),
        tile_col.reshape(slots),
        info,
        gather_sources(features.T),
        node_dev,
    )
    agg = reduce_rows(*parts)
    hidden = jnp.dot(agg, weight, preferred_element_type=jnp.float32) + bias
    return jax.nn.relu(hidden).astype(jnp.bfloat16)


def solution(mesh):
    fine = Mesh(mesh.devices.reshape(4, 2, 2, 2, 4), NAMES)
    row, col = ("rz", "ry"), ("cy", "cc")
    placed = (
        P(row + col, "fx"),
        P(row, col, "fx", None, None),
        P(row, col, "fx"),
        P(row, col, "fx"),
        P(row, col, "fx"),
        P(),
        P(),
    )
    return jax.shard_map(
        body, mesh=fine, in_specs=placed, out_specs=P(NAMES, None), check_vma=False
    )
```
